32 devices in a mesh: seq: 16 (over z, y, core), head: 2 (over x).
Axes of the slice: x: 2, y: 2, z: 4, core: 2. Of those that a mesh axis runs over, the one named last changes fastest.
Arguments:
- queries: bfloat16 [8192, 4096], P(('seq', 'head')), may hold values from -6 to 6
- key_vectors: bfloat16 [8192, 4096], P(('seq', 'head')), may hold values from -6 to 6
- value_vectors: bfloat16 [8192, 4096], P(('seq', 'head')), may hold values from -6 to 6
- out_grads: bfloat16 [8192, 4096], P(('seq', 'head')), may hold values from -6 to 6
Outputs:
- grad_queries: bfloat16 [8192, 4096], P('seq', 'head')
- grad_keys: bfloat16 [8192, 4096], P('seq', 'head')
- grad_values: bfloat16 [8192, 4096], P('seq', 'head')
The draws below stay inside these ranges and needn't reach their ends.
All inputs are finite; a program needn't handle non-finite values.
Results may differ from the reference program's by a relative error of at most 0.0051.
Values may be sent and summed in bfloat16 or wider, within the bound.
No kernel may reach another device: no remote copies, remote signals or barrier semaphores. Data moves between devices by JAX's collectives and lax.ppermute only.
A program may use at most 192 MiB of HBM per device.

```python
import jax
import jax.numpy as jnp
from jax import lax

HEADS = 32
DK = 128
BLOCK = 512
TOKENS = 8192


def levels(key, extent, shards, smallest, top_value):
    factor_of = 1.0
    for position, shards_of in shards:
        steps = jax.random.uniform(jax.random.fold_in(jax.random.fold_in(key, 6), position), (shards_of,), jnp.float32, smallest / len(shards), top_value / len(shards))
        factor_of = factor_of * jnp.repeat(jnp.exp(steps), extent[position] // shards_of).reshape((-1,) + (1,) * (len(extent) - 1 - position))
    return factor_of


def centred(stream_key, extent, deviation, most, pieces=(), dtype=jnp.bfloat16):
    values = jax.random.normal(stream_key, extent, jnp.float32) * deviation
    if len(pieces) > 0:
        values = levels(stream_key, extent, pieces, -0.22, 0.18) * values
    return jnp.clip(values, min=-most, max=most).astype(dtype)


def setup_inputs(seed: int = 0) -> dict:
    key_of = jax.random.split(jax.random.key(seed), 5)
    return {
        "queries": centred(key_of[0], (TOKENS, HEADS * DK), 1.0, 6.0, ((0, 32),)),
        "key_vectors": centred(key_of[1], (TOKENS, HEADS * DK), 1.0, 6.0, ((0, 32),)),
        "value_vectors": centred(key_of[2], (TOKENS, HEADS * DK), 1.0, 6.0, ((0, 32),)),
        "out_grads": centred(key_of[3], (TOKENS, HEADS * DK), 1.0, 6.0, ((0, 32),)),
    }


def rounded(values):
    return lax.optimization_barrier(values.astype(jnp.bfloat16)).astype(jnp.float32)


def head_grads(pack):
    query_b, key_b, value_b, grad_b = pack
    q32 = query_b.astype(jnp.float32)
    k32 = key_b.astype(jnp.float32)
    v32 = value_b.astype(jnp.float32)
    g32 = grad_b.astype(jnp.float32)
    lower = jnp.tril(jnp.ones((BLOCK, BLOCK), jnp.float32))
    probe = rounded(jnp.einsum('nta,nsa->nts', g32, v32) * lower)
    affin = rounded(jnp.einsum('nta,nsa->nts', q32, k32) * lower)
    kv_state = jnp.einsum('nsa,nsb->nab', k32, v32)
    qg_state = jnp.einsum('nta,ntb->nab', q32, g32)
    prefix = rounded(jnp.cumsum(kv_state, axis=0) - kv_state)
    suffix = rounded(jnp.sum(qg_state, axis=0, keepdims=True) - jnp.cumsum(qg_state, axis=0))
    scale = 1.0 / (DK * TOKENS) ** 0.5
    dq = jnp.einsum('nts,nsa->nta', probe, k32) + jnp.einsum('ntb,nab->nta', g32, prefix)
    dk = jnp.einsum('nts,nta->nsa', probe, q32) + jnp.einsum('nsb,nab->nsa', v32, suffix)
    dv = jnp.einsum('nts,ntb->nsb', affin, g32) + jnp.einsum('nsa,nab->nsb', k32, suffix)
    return ((scale * dq).astype(jnp.bfloat16), (scale * dk).astype(jnp.bfloat16), (scale * dv).astype(jnp.bfloat16))


def split_heads(array):
    return jnp.transpose(array.reshape(TOKENS // BLOCK, BLOCK, HEADS, DK), (2, 0, 1, 3))


def join_heads(array):
    return jnp.transpose(array, (1, 2, 0, 3)).reshape(TOKENS, HEADS * DK)


def reference(queries, key_vectors, value_vectors, out_grads):
    pack = (split_heads(queries), split_heads(key_vectors), split_heads(value_vectors), split_heads(out_grads))
    dq, dk, dv = lax.map(head_grads, pack)
    return (join_heads(dq), join_heads(dk), join_heads(dv))
```

```python
import functools
import math

import jax
import jax.numpy as jnp
from jax import lax
from jax.experimental import pallas as pl
from jax.experimental.pallas import tpu as pltpu
from jax.sharding import PartitionSpec as P

DK = 128
F32 = jnp.float32
BF16 = jnp.bfloat16
WIRE = jnp.bfloat16


NT = (((1,), (1,)), ((), ()))
TN = (((0,), (0,)), ((), ()))
NN = (((1,), (0,)), ((), ()))


def mm(a, b, dims):
    return lax.dot_general(a, b, dims, preferred_element_type=F32)


def cost(flops, size):
    return pl.CostEstimate(flops=flops, bytes_accessed=size, transcendentals=0)


def pack_kernel(col_ref, q_ref, k_ref, v_ref, g_ref, out_ref):
    out_ref[0] = q_ref[...]
    out_ref[1] = k_ref[...]
    out_ref[2] = v_ref[...]
    out_ref[3] = g_ref[...]


def pack(col, arrays, heads):
    rows = arrays[0].shape[0]
    own = pl.BlockSpec((rows, DK), lambda i, c: (0, c[0] + i))
    return pl.pallas_call(
        pack_kernel,
        grid_spec=pltpu.PrefetchScalarGridSpec(
            num_scalar_prefetch=1,
            grid=(heads,),
            in_specs=[own] * 4,
            out_specs=pl.BlockSpec((4, rows, DK), lambda i, c: (0, 0, i)),
        ),
        out_shape=jax.ShapeDtypeStruct((4, rows, heads * DK), BF16),
        cost_estimate=cost(0, 16 * rows * heads * DK),
        name="pack",
    )(col, *arrays)


def state_kernel(peers, col_ref, q_ref, k_ref, v_ref, g_ref, *rest):
    out_ref = rest[peers]
    kv = mm(k_ref[...], v_ref[...], TN)
    qg = mm(q_ref[...], g_ref[...], TN)
    for r in rest[:peers]:
        kv = kv + mm(r[1], r[2], TN)
        qg = qg + mm(r[0], r[3], TN)
    out_ref[0, 0] = kv.astype(out_ref.dtype)
    out_ref[1, 0] = qg.astype(out_ref.dtype)


def states(col, arrays, got, heads, dtype):
    rows = arrays[0].shape[0]
    own = pl.BlockSpec((rows, DK), lambda i, c: (0, c[0] + i))
    there = pl.BlockSpec((4, rows, DK), lambda i, c: (0, 0, i))
    tokens = rows * (1 + len(got))
    return pl.pallas_call(
        functools.partial(state_kernel, len(got)),
        grid_spec=pltpu.PrefetchScalarGridSpec(
            num_scalar_prefetch=1,
            grid=(heads,),
            in_specs=[own] * 4 + [there] * len(got),
            out_specs=pl.BlockSpec((2, 1, DK, DK), lambda i, c: (0, i, 0, 0)),
        ),
        out_shape=jax.ShapeDtypeStruct((2, heads, DK, DK), dtype),
        cost_estimate=cost(4 * tokens * DK * DK * heads, 8 * tokens * heads * DK),
        name="states",
    )(col, *arrays, *got)


def out_kernel(peers, aliased, scale, col_ref, src_ref, q_ref, k_ref, v_ref, g_ref, *rest):
    got = rest[:peers]
    pre_ref, suf_ref = rest[peers : peers + 2]
    skip = peers + 2 + 3 * aliased
    dq_ref, dk_ref, dv_ref, all_ref = rest[skip : skip + 4]
    rows = q_ref.shape[0]
    mine = pl.multiple_of(src_ref[0] * rows, rows)
    for j, ref in enumerate((q_ref, k_ref, v_ref, g_ref)):
        all_ref[j, pl.ds(mine, rows), :] = ref[...]
    for p, r in enumerate(got):
        at = pl.multiple_of(src_ref[p + 1] * rows, rows)
        for j in range(4):
            all_ref[j, pl.ds(at, rows), :] = r[j]
    total = all_ref.shape[1]
    half = total // 2
    up, down = slice(0, half), slice(half, total)
    q_a, q_b = all_ref[0, up, :], all_ref[0, down, :]
    k_a, k_b = all_ref[1, up, :], all_ref[1, down, :]
    v_a, v_b = all_ref[2, up, :], all_ref[2, down, :]
    g_a, g_b = all_ref[3, up, :], all_ref[3, down, :]
    row = lax.broadcasted_iota(jnp.int32, (half, half), 0)
    column = lax.broadcasted_iota(jnp.int32, (half, half), 1)
    lower, upper = row >= column, row <= column

    def tri(x, keep):
        return jnp.where(keep, x, 0.0).astype(BF16)

    pre, suf = pre_ref[0], suf_ref[0]
    dq_a = mm(tri(mm(g_a, v_a, NT), lower), k_a, NN) + mm(g_a, pre, NT)
    dq_b = (
        mm(mm(g_b, v_a, NT).astype(BF16), k_a, NN)
        + mm(tri(mm(g_b, v_b, NT), lower), k_b, NN)
        + mm(g_b, pre, NT)
    )
    dq_ref[up, :] = (scale * dq_a).astype(BF16)
    dq_ref[down, :] = (scale * dq_b).astype(BF16)
    dk_a = (
        mm(tri(mm(v_a, g_a, NT), upper), q_a, NN)
        + mm(mm(v_a, g_b, NT).astype(BF16), q_b, NN)
        + mm(v_a, suf, NT)
    )
    dk_b = mm(tri(mm(v_b, g_b, NT), upper), q_b, NN) + mm(v_b, suf, NT)
    dk_ref[up, :] = (scale * dk_a).astype(BF16)
    dk_ref[down, :] = (scale * dk_b).astype(BF16)
    dv_a = (
        mm(tri(mm(k_a, q_a, NT), upper), g_a, NN)
        + mm(mm(k_a, q_b, NT).astype(BF16), g_b, NN)
        + mm(k_a, suf, NN)
    )
    dv_b = mm(tri(mm(k_b, q_b, NT), upper), g_b, NN) + mm(k_b, suf, NN)
    dv_ref[up, :] = (scale * dv_a).astype(BF16)
    dv_ref[down, :] = (scale * dv_b).astype(BF16)


def outputs(col, src, arrays, got, pre, suf, first_state, first, heads, heads_here, scale, outs):
    rows = arrays[0].shape[0]
    total = rows * (1 + len(got))
    own = pl.BlockSpec((rows, DK), lambda i, c, s: (0, c[0] + i))
    there = pl.BlockSpec((4, rows, DK), lambda i, c, s: (0, 0, i))
    state = pl.BlockSpec((1, DK, DK), lambda i, c, s: (first_state + i, 0, 0))
    here = pl.BlockSpec((total, DK), lambda i, c, s: (0, first + i))
    aliased = outs is not None
    base = 2 + 4 + len(got) + 2
    return pl.pallas_call(
        functools.partial(out_kernel, len(got), int(aliased), scale),
        grid_spec=pltpu.PrefetchScalarGridSpec(
            num_scalar_prefetch=2,
            grid=(heads,),
            in_specs=[own] * 4
            + [there] * len(got)
            + [state] * 2
            + ([pl.BlockSpec(memory_space=pl.ANY)] * 3 if aliased else []),
            out_specs=[here] * 3,
            scratch_shapes=[pltpu.VMEM((4, total, DK), BF16)],
        ),
        out_shape=[jax.ShapeDtypeStruct((total, heads_here * DK), BF16)] * 3,
        input_output_aliases={base + j: j for j in range(3)} if aliased else {},
        cost_estimate=cost(14 * total * total * DK * heads, 14 * total * DK * heads),
        name="outputs",
    )(col, src, *arrays, *got, pre, suf, *(outs if aliased else ()))


def scan(own):
    count = lax.axis_size("seq")
    chips = count // 2
    core = lax.axis_index("seq") % 2
    swap = [(i, i ^ 1) for i in range(count)]
    other = lax.ppermute(own.astype(WIRE), "seq", swap).astype(F32)
    chip = own + other
    mine = jnp.where(core == 0, chip[0], chip[1])
    total = mine
    step = 1
    while step < chips:
        pairs = [(2 * c, 2 * (c + step)) for c in range(chips - step)]
        pairs += [(2 * (c + step) + 1, 2 * c + 1) for c in range(chips - step)]
        total = total + lax.ppermute(total.astype(WIRE), "seq", pairs).astype(F32)
        step *= 2
    enter = total - mine
    kept = enter.astype(BF16)
    given = (enter + jnp.where(core == 0, own[0], own[1])).astype(BF16)
    taken = lax.ppermute(given, "seq", swap)
    return jnp.where(core == 0, kept, taken), jnp.where(core == 0, taken, kept)


def local(queries, key_vectors, value_vectors, out_grads):
    arrays = (queries, key_vectors, value_vectors, out_grads)
    peers = lax.axis_size("head")
    place = lax.axis_index("head")
    rows = queries.shape[0]
    heads_here = queries.shape[1] // DK // peers
    total_tokens = rows * peers * lax.axis_size("seq")
    scale = 1.0 / math.sqrt(DK * total_tokens)
    unit = heads_here // 8
    sizes = [unit, 3 * unit, 2 * unit, heads_here - 6 * unit]
    firsts = [sum(sizes[:i]) for i in range(4)]

    def column(shift, first):
        return ((place + shift) % peers * heads_here + first).astype(jnp.int32).reshape(1)

    def move(value, shift):
        return lax.ppermute(value, "head", [(i, (i + shift) % peers) for i in range(peers)])

    shifts = range(1, peers)
    src = jnp.stack([place] + [(place - s) % peers for s in shifts]).astype(jnp.int32)

    def exchange(c):
        return [move(pack(column(s, firsts[c]), arrays, sizes[c]), s) for s in shifts]

    got = [None] * 4
    got[0] = exchange(0)
    late_sent = [move(states(column(s, firsts[3]), arrays, [], sizes[3], BF16), s) for s in shifts]
    late = states(column(0, firsts[3]), arrays, [], sizes[3], F32)
    for c in (1, 2, 3):
        got[c] = exchange(c)
    for piece in late_sent:
        late = late + piece.astype(F32)
    own = [states(column(0, firsts[c]), arrays, got[c], sizes[c], F32) for c in range(3)]
    pre_a, suf_a = scan(jnp.concatenate([own[0], own[1], late], axis=1))
    pre_b, suf_b = scan(own[2])

    outs = None
    at = [0, sizes[0], 0, sizes[0] + sizes[1]]
    for c in (0, 1, 2, 3):
        pre, suf = (pre_b, suf_b) if c == 2 else (pre_a, suf_a)
        outs = outputs(
            column(0, firsts[c]), src, arrays, got[c], pre, suf, at[c], firsts[c], sizes[c], heads_here, scale, outs
        )
    return tuple(outs)


def solution(mesh):
    tokens = P(("seq", "head"), None)
    return jax.shard_map(
        local,
        mesh=mesh,
        in_specs=(tokens,) * 4,
        out_specs=(P("seq", "head"),) * 3,
        check_vma=False,
    )
```

```python
import functools
import math

import jax
import jax.numpy as jnp
from jax import lax
from jax.experimental import pallas as pl
from jax.experimental.pallas import tpu as pltpu
from jax.sharding import PartitionSpec as P


DK = 128
F32 = jnp.float32
BF16 = jnp.bfloat16
PAIR = 2 * DK


NT = (((1,), (1,)), ((), ()))
TN = (((0,), (0,)), ((), ()))
NN = (((1,), (0,)), ((), ()))


def mm(a, b, dims):
    return lax.dot_general(a, b, dims, preferred_element_type=F32)


def cost(flops, size):
    return pl.CostEstimate(flops=flops, bytes_accessed=size, transcendentals=0)


def pack_kernel(col_ref, q_ref, k_ref, v_ref, g_ref, out_ref):
    out_ref[0] = q_ref[...]
    out_ref[1] = k_ref[...]
    out_ref[2] = v_ref[...]
    out_ref[3] = g_ref[...]


def pack(col, arrays, first, pairs):
    rows = arrays[0].shape[0]
    own = pl.BlockSpec((rows, PAIR), lambda i, c: (0, c[0] + first + i))
    return pl.pallas_call(
        pack_kernel,
        grid_spec=pltpu.PrefetchScalarGridSpec(
            num_scalar_prefetch=1,
            grid=(pairs,),
            in_specs=[own] * 4,
            out_specs=pl.BlockSpec((4, rows, PAIR), lambda i, c: (0, 0, i)),
        ),
        out_shape=jax.ShapeDtypeStruct((4, rows, pairs * PAIR), BF16),
        cost_estimate=cost(0, 16 * rows * pairs * PAIR),
        name="pack",
    )(col, *arrays)


def state_kernel(peers, col_ref, q_ref, k_ref, v_ref, g_ref, *rest):
    out_ref = rest[peers]
    for j in range(PAIR // DK):
        at = slice(j * DK, (j + 1) * DK)
        kv = mm(k_ref[:, at], v_ref[:, at], TN)
        qg = mm(q_ref[:, at], g_ref[:, at], TN)
        for r in rest[:peers]:
            kv = kv + mm(r[1, :, at], r[2, :, at], TN)
            qg = qg + mm(r[0, :, at], r[3, :, at], TN)
        out_ref[0, j] = kv.astype(out_ref.dtype)
        out_ref[1, j] = qg.astype(out_ref.dtype)


def states(col, arrays, got, first, pairs, dtype):
    rows = arrays[0].shape[0]
    own = pl.BlockSpec((rows, PAIR), lambda i, c: (0, c[0] + first + i))
    there = pl.BlockSpec((4, rows, PAIR), lambda i, c: (0, 0, i))
    tokens = rows * (1 + len(got))
    per = PAIR // DK
    return pl.pallas_call(
        functools.partial(state_kernel, len(got)),
        grid_spec=pltpu.PrefetchScalarGridSpec(
            num_scalar_prefetch=1,
            grid=(pairs,),
            in_specs=[own] * 4 + [there] * len(got),
            out_specs=pl.BlockSpec((2, per, DK, DK), lambda i, c: (0, i, 0, 0)),
        ),
        out_shape=jax.ShapeDtypeStruct((2, per * pairs, DK, DK), dtype),
        cost_estimate=cost(4 * tokens * DK * PAIR * pairs, 8 * tokens * pairs * PAIR),
        name="states",
    )(col, *arrays, *got)


def out_kernel(peers, aliased, scale, col_ref, src_ref, q_ref, k_ref, v_ref, g_ref, *rest):
    got = rest[:peers]
    pre_ref, suf_ref = rest[peers : peers + 2]
    skip = peers + 2 + 3 * aliased
    dq_ref, dk_ref, dv_ref, all_ref = rest[skip : skip + 4]
    rows = q_ref.shape[0]
    mine = pl.multiple_of(src_ref[0] * rows, rows)
    for j, ref in enumerate((q_ref, k_ref, v_ref, g_ref)):
        all_ref[j, pl.ds(mine, rows), :] = ref[...]
    for p, r in enumerate(got):
        at = pl.multiple_of(src_ref[p + 1] * rows, rows)
        for j in range(4):
            all_ref[j, pl.ds(at, rows), :] = r[j]
    total = all_ref.shape[1]
    half = total // 2
    up, down = slice(0, half), slice(half, total)
    row = lax.broadcasted_iota(jnp.int32, (half, half), 0)
    column = lax.broadcasted_iota(jnp.int32, (half, half), 1)
    lower, upper = row >= column, row <= column

    def tri(x, keep):
        return jnp.where(keep, x, 0.0).astype(BF16)

    for j in range(PAIR // DK):
        at = slice(j * DK, (j + 1) * DK)
        q_a, q_b = all_ref[0, up, at], all_ref[0, down, at]
        k_a, k_b = all_ref[1, up, at], all_ref[1, down, at]
        v_a, v_b = all_ref[2, up, at], all_ref[2, down, at]
        g_a, g_b = all_ref[3, up, at], all_ref[3, down, at]
        pre, suf = pre_ref[j], suf_ref[j]
        dq_a = mm(tri(mm(g_a, v_a, NT), lower), k_a, NN) + mm(g_a, pre, NT)
        dq_b = (
            mm(mm(g_b, v_a, NT).astype(BF16), k_a, NN)
            + mm(tri(mm(g_b, v_b, NT), lower), k_b, NN)
            + mm(g_b, pre, NT)
        )
        dq_ref[up, at] = (scale * dq_a).astype(BF16)
        dq_ref[down, at] = (scale * dq_b).astype(BF16)
        dk_a = (
            mm(tri(mm(v_a, g_a, NT), upper), q_a, NN)
            + mm(mm(v_a, g_b, NT).astype(BF16), q_b, NN)
            + mm(v_a, suf, NT)
        )
        dk_b = mm(tri(mm(v_b, g_b, NT), upper), q_b, NN) + mm(v_b, suf, NT)
        dk_ref[up, at] = (scale * dk_a).astype(BF16)
        dk_ref[down, at] = (scale * dk_b).astype(BF16)
        dv_a = (
            mm(tri(mm(k_a, q_a, NT), upper), g_a, NN)
            + mm(mm(k_a, q_b, NT).astype(BF16), g_b, NN)
            + mm(k_a, suf, NN)
        )
        dv_b = mm(tri(mm(k_b, q_b, NT), upper), g_b, NN) + mm(k_b, suf, NN)
        dv_ref[up, at] = (scale * dv_a).astype(BF16)
        dv_ref[down, at] = (scale * dv_b).astype(BF16)


def outputs(col, src, arrays, got, pre, suf, first_state, first, pairs, heads_here, scale, outs):
    rows = arrays[0].shape[0]
    total = rows * (1 + len(got))
    own = pl.BlockSpec((rows, PAIR), lambda i, c, s: (0, c[0] + first + i))
    there = pl.BlockSpec((4, rows, PAIR), lambda i, c, s: (0, 0, i))
    state = pl.BlockSpec((PAIR // DK, DK, DK), lambda i, c, s: (first_state + i, 0, 0))
    here = pl.BlockSpec((total, PAIR), lambda i, c, s: (0, first + i))
    aliased = outs is not None
    base = 2 + 4 + len(got) + 2
    return pl.pallas_call(
        functools.partial(out_kernel, len(got), int(aliased), scale),
        grid_spec=pltpu.PrefetchScalarGridSpec(
            num_scalar_prefetch=2,
            grid=(pairs,),
            in_specs=[own] * 4
            + [there] * len(got)
            + [state] * 2
            + ([pl.BlockSpec(memory_space=pl.ANY)] * 3 if aliased else []),
            out_specs=[here] * 3,
            scratch_shapes=[pltpu.VMEM((4, total, PAIR), BF16)],
        ),
        out_shape=[jax.ShapeDtypeStruct((total, heads_here * DK), BF16)] * 3,
        input_output_aliases={base + j: j for j in range(3)} if aliased else {},
        cost_estimate=cost(14 * total * total * PAIR * pairs, 14 * total * PAIR * pairs),
        name="outputs",
    )(col, src, *arrays, *got, pre, suf, *(outs if aliased else ()))


def scan(own, sent):
    count = lax.axis_size("seq")
    chips = count // 2
    core = lax.axis_index("seq") % 2
    swap = [(i, i ^ 1) for i in range(count)]
    other = lax.ppermute(sent, "seq", swap).astype(F32)
    chip = own + other
    mine = jnp.where(core == 0, chip[0], chip[1])
    total = mine
    step = 1
    while step < chips:
        pairs = [(2 * c, 2 * (c + step)) for c in range(chips - step)]
        pairs += [(2 * (c + step) + 1, 2 * c + 1) for c in range(chips - step)]
        total = total + lax.ppermute(total.astype(BF16), "seq", pairs).astype(F32)
        step *= 2
    enter = total - mine
    kept = enter.astype(BF16)
    given = (enter + jnp.where(core == 0, own[0], own[1])).astype(BF16)
    taken = lax.ppermute(given, "seq", swap)
    return jnp.where(core == 0, kept, taken), jnp.where(core == 0, taken, kept)


def local(queries, key_vectors, value_vectors, out_grads):
    return grads((queries, key_vectors, value_vectors, out_grads))


def grads(arrays):
    peers = lax.axis_size("head")
    place = lax.axis_index("head")
    rows = arrays[0].shape[0]
    heads_here = arrays[0].shape[1] // DK // peers
    pairs_here = heads_here * DK // PAIR
    total_tokens = rows * peers * lax.axis_size("seq")
    scale = 1.0 / math.sqrt(DK * total_tokens)
    late = -(-3 * pairs_here // 8)
    early = pairs_here - late
    sizes = [1, (early - 1) // 2, early - 1 - (early - 1) // 2, late - late // 3, late // 3]
    sizes = [n for n in sizes if n]
    firsts = [sum(sizes[:i]) for i in range(len(sizes))]
    chunks = range(len(sizes))
    split = firsts.index(early)
    shifts = range(1, peers)
    cols = [((place + s) % peers * pairs_here).astype(jnp.int32).reshape(1) for s in range(peers)]
    src = jnp.stack([(place - s) % peers for s in range(peers)]).astype(jnp.int32)

    def move(value, shift):
        return lax.ppermute(value, "head", [(i, (i + shift) % peers) for i in range(peers)])

    def exchange(c):
        return [move(pack(cols[s], arrays, firsts[c], sizes[c]), s) for s in shifts]

    got = {0: exchange(0)}
    late_sent = [move(states(cols[s], arrays, [], early, late, BF16), s) for s in shifts]
    for c in chunks[1:]:
        got[c] = exchange(c)
    late_own = states(cols[0], arrays, [], early, late, F32)
    for piece in late_sent:
        late_own = late_own + piece.astype(F32)
    own = []
    for c in chunks[:split]:
        own.append(states(cols[0], arrays, got[c], firsts[c], sizes[c], F32))
    own[0] = jnp.concatenate([own[0], late_own], axis=1)
    scanned = [scan(own[c], own[c].astype(BF16)) for c in chunks[:split]]

    outs = None
    order = [*chunks[: split - 1], split, split - 1, *chunks[split + 1 :]]
    for c in order:
        pre, suf = scanned[c if c < split else 0]
        at = 0 if c < split else sizes[0] + firsts[c] - early
        outs = outputs(
            cols[0], src, arrays, got[c], pre, suf, at, firsts[c], sizes[c], heads_here, scale, outs
        )
    return tuple(outs)


def solution(mesh):
    tokens = P(("seq", "head"), None)
    return jax.shard_map(
        local,
        mesh=mesh,
        in_specs=(tokens,) * 4,
        out_specs=(P("seq", "head"),) * 3,
        check_vma=False,
    )
```

```python
import functools
import math

import jax
import jax.numpy as jnp
from jax import lax
from jax.experimental import pallas as pl
from jax.experimental.pallas import tpu as pltpu
from jax.sharding import PartitionSpec as P


DK = 128
F32 = jnp.float32
BF16 = jnp.bfloat16
PAIR = 2 * DK


NT = (((1,), (1,)), ((), ()))
TN = (((0,), (0,)), ((), ()))
NN = (((1,), (0,)), ((), ()))


def mm(a, b, dims):
    return lax.dot_general(a, b, dims, preferred_element_type=F32)


def cost(flops, size):
    return pl.CostEstimate(flops=flops, bytes_accessed=size, transcendentals=0)


def pack_kernel(bounds, peers, col_ref, *refs):
    at = pl.program_id(0)
    ins, outs = refs[: 4 * (peers - 1)], refs[4 * (peers - 1) :]
    for c, (low, high) in enumerate(bounds):

        @pl.when((at >= low) & (at < high))
        def _():
            for s in range(peers - 1):
                for j in range(4):
                    outs[c * (peers - 1) + s][j] = ins[4 * s + j][...]


def pack(cols, peers, arrays, first, sizes):
    rows = arrays[0].shape[0]
    bounds = [(sum(sizes[:i]), sum(sizes[: i + 1])) for i in range(len(sizes))]

    def own(s):
        return pl.BlockSpec((rows, PAIR), lambda i, c: (0, c[s] + first + i))

    def there(low, high):
        return pl.BlockSpec((4, rows, PAIR), lambda i, c: (0, 0, jnp.clip(i - low, 0, high - low - 1)))

    total = sum(sizes)
    flat = pl.pallas_call(
        functools.partial(pack_kernel, bounds, peers),
        grid_spec=pltpu.PrefetchScalarGridSpec(
            num_scalar_prefetch=1,
            grid=(total,),
            in_specs=[own(s) for s in range(1, peers) for _ in range(4)],
            out_specs=[there(*at) for at in bounds for _ in range(1, peers)],
        ),
        out_shape=[
            jax.ShapeDtypeStruct((4, rows, n * PAIR), BF16) for n in sizes for _ in range(1, peers)
        ],
        cost_estimate=cost(0, 16 * rows * total * PAIR * (peers - 1)),
        name="pack",
    )(cols, *(list(arrays) * (peers - 1)))
    return [flat[i * (peers - 1) : (i + 1) * (peers - 1)] for i in range(len(sizes))]


def state_kernel(peers, col_ref, q_ref, k_ref, v_ref, g_ref, *rest):
    out_ref = rest[peers]
    for j in range(PAIR // DK):
        at = slice(j * DK, (j + 1) * DK)
        kv = mm(k_ref[:, at], v_ref[:, at], TN)
        qg = mm(q_ref[:, at], g_ref[:, at], TN)
        for r in rest[:peers]:
            kv = kv + mm(r[1, :, at], r[2, :, at], TN)
            qg = qg + mm(r[0, :, at], r[3, :, at], TN)
        out_ref[0, j] = kv.astype(out_ref.dtype)
        out_ref[1, j] = qg.astype(out_ref.dtype)


def states(cols, arrays, got, first, pairs):
    rows = arrays[0].shape[0]
    own = pl.BlockSpec((rows, PAIR), lambda i, c: (0, c[0] + first + i))
    there = pl.BlockSpec((4, rows, PAIR), lambda i, c: (0, 0, i))
    tokens = rows * (1 + len(got))
    per = PAIR // DK
    return pl.pallas_call(
        functools.partial(state_kernel, len(got)),
        grid_spec=pltpu.PrefetchScalarGridSpec(
            num_scalar_prefetch=1,
            grid=(pairs,),
            in_specs=[own] * 4 + [there] * len(got),
            out_specs=pl.BlockSpec((2, per, DK, DK), lambda i, c: (0, i, 0, 0)),
        ),
        out_shape=jax.ShapeDtypeStruct((2, per * pairs, DK, DK), BF16),
        cost_estimate=cost(4 * tokens * DK * PAIR * pairs, 8 * tokens * pairs * PAIR),
        name="states",
    )(cols, *arrays, *got)


def source_kernel(peers, col_ref, *refs):
    for s in range(peers):
        q_ref, k_ref, v_ref, g_ref = refs[4 * s : 4 * s + 4]
        out_ref = refs[4 * peers + s]
        for j in range(PAIR // DK):
            at = slice(j * DK, (j + 1) * DK)
            out_ref[0, j] = mm(k_ref[:, at], v_ref[:, at], TN).astype(out_ref.dtype)
            out_ref[1, j] = mm(q_ref[:, at], g_ref[:, at], TN).astype(out_ref.dtype)


def source_states(cols, peers, arrays, first, pairs):
    rows = arrays[0].shape[0]
    per = PAIR // DK

    def own(s):
        return pl.BlockSpec((rows, PAIR), lambda i, c: (0, c[s] + first + i))

    return pl.pallas_call(
        functools.partial(source_kernel, peers),
        grid_spec=pltpu.PrefetchScalarGridSpec(
            num_scalar_prefetch=1,
            grid=(pairs,),
            in_specs=[own(s) for s in range(peers) for _ in range(4)],
            out_specs=[pl.BlockSpec((2, per, DK, DK), lambda i, c: (0, i, 0, 0))] * peers,
        ),
        out_shape=[
            jax.ShapeDtypeStruct((2, per * pairs, DK, DK), F32 if s == 0 else BF16) for s in range(peers)
        ],
        cost_estimate=cost(4 * rows * peers * DK * PAIR * pairs, 8 * rows * peers * pairs * PAIR),
        name="source_states",
    )(cols, *(list(arrays) * peers))


def out_kernel(peers, aliased, scale, col_ref, src_ref, q_ref, k_ref, v_ref, g_ref, *rest):
    got = rest[:peers]
    sum_ref = rest[peers]
    skip = peers + 1 + 3 * aliased
    dq_ref, dk_ref, dv_ref, all_ref = rest[skip : skip + 4]
    rows = q_ref.shape[0]
    mine = pl.multiple_of(src_ref[0] * rows, rows)
    for j, ref in enumerate((q_ref, k_ref, v_ref, g_ref)):
        all_ref[j, pl.ds(mine, rows), :] = ref[...]
    for p, r in enumerate(got):
        at = pl.multiple_of(src_ref[p + 1] * rows, rows)
        for j in range(4):
            all_ref[j, pl.ds(at, rows), :] = r[j]
    total = all_ref.shape[1]
    half = total // 2
    up, down = slice(0, half), slice(half, total)
    row = lax.broadcasted_iota(jnp.int32, (half, half), 0)
    column = lax.broadcasted_iota(jnp.int32, (half, half), 1)
    lower, upper = row >= column, row <= column

    def tri(x, keep):
        return jnp.where(keep, x, 0.0).astype(BF16)

    for j in range(PAIR // DK):
        at = slice(j * DK, (j + 1) * DK)
        q_a, q_b = all_ref[0, up, at], all_ref[0, down, at]
        k_a, k_b = all_ref[1, up, at], all_ref[1, down, at]
        v_a, v_b = all_ref[2, up, at], all_ref[2, down, at]
        g_a, g_b = all_ref[3, up, at], all_ref[3, down, at]
        pre, suf = sum_ref[0, j], sum_ref[1, j]
        dq_a = mm(tri(mm(g_a, v_a, NT), lower), k_a, NN) + mm(g_a, pre, NT)
        dq_b = (
            mm(mm(g_b, v_a, NT).astype(BF16), k_a, NN)
            + mm(tri(mm(g_b, v_b, NT), lower), k_b, NN)
            + mm(g_b, pre, NT)
        )
        dq_ref[up, at] = (scale * dq_a).astype(BF16)
        dq_ref[down, at] = (scale * dq_b).astype(BF16)
        dk_a = (
            mm(tri(mm(v_a, g_a, NT), upper), q_a, NN)
            + mm(mm(v_a, g_b, NT).astype(BF16), q_b, NN)
            + mm(v_a, suf, NT)
        )
        dk_b = mm(tri(mm(v_b, g_b, NT), upper), q_b, NN) + mm(v_b, suf, NT)
        dk_ref[up, at] = (scale * dk_a).astype(BF16)
        dk_ref[down, at] = (scale * dk_b).astype(BF16)
        dv_a = (
            mm(tri(mm(k_a, q_a, NT), upper), g_a, NN)
            + mm(mm(k_a, q_b, NT).astype(BF16), g_b, NN)
            + mm(k_a, suf, NN)
        )
        dv_b = mm(tri(mm(k_b, q_b, NT), upper), g_b, NN) + mm(k_b, suf, NN)
        dv_ref[up, at] = (scale * dv_a).astype(BF16)
        dv_ref[down, at] = (scale * dv_b).astype(BF16)


def outputs(cols, src, arrays, got, sums, first_sum, first, pairs, heads_here, scale, outs):
    rows = arrays[0].shape[0]
    total = rows * (1 + len(got))
    own = pl.BlockSpec((rows, PAIR), lambda i, c, s: (0, c[0] + first + i))
    there = pl.BlockSpec((4, rows, PAIR), lambda i, c, s: (0, 0, i))
    state = pl.BlockSpec((2, PAIR // DK, DK, DK), lambda i, c, s: (0, first_sum + i, 0, 0))
    here = pl.BlockSpec((total, PAIR), lambda i, c, s: (0, first + i))
    aliased = outs is not None
    base = 2 + 4 + len(got) + 1
    return pl.pallas_call(
        functools.partial(out_kernel, len(got), int(aliased), scale),
        grid_spec=pltpu.PrefetchScalarGridSpec(
            num_scalar_prefetch=2,
            grid=(pairs,),
            in_specs=[own] * 4
            + [there] * len(got)
            + [state]
            + ([pl.BlockSpec(memory_space=pl.ANY)] * 3 if aliased else []),
            out_specs=[here] * 3,
            scratch_shapes=[pltpu.VMEM((4, total, PAIR), BF16)],
        ),
        out_shape=[jax.ShapeDtypeStruct((total, heads_here * DK), BF16)] * 3,
        input_output_aliases={base + j: j for j in range(3)} if aliased else {},
        cost_estimate=cost(14 * total * total * PAIR * pairs, 14 * total * PAIR * pairs),
        name="outputs",
    )(cols, src, *arrays, *got, sums, *(outs if aliased else ()))


def scan(own):
    count = lax.axis_size("seq")
    part = own.reshape(count, -1, DK)
    parts = lax.all_to_all(part, "seq", 0, 0, tiled=True).astype(F32)
    running, before = jnp.zeros_like(parts[0]), []
    for i in range(count):
        before.append(running)
        running = running + parts[i]
    before = jnp.stack(before)
    after = running[None] - before - parts
    mine = jnp.where(lax.axis_index("seq") < count // 2, before, after).astype(BF16)
    return lax.all_to_all(mine, "seq", 0, 0, tiled=True).reshape(own.shape)


def local(queries, key_vectors, value_vectors, out_grads):
    return grads((queries, key_vectors, value_vectors, out_grads))


def grads(arrays):
    peers = lax.axis_size("head")
    place = lax.axis_index("head")
    rows = arrays[0].shape[0]
    heads_here = arrays[0].shape[1] // DK // peers
    pairs_here = heads_here * DK // PAIR
    total_tokens = rows * peers * lax.axis_size("seq")
    scale = 1.0 / math.sqrt(DK * total_tokens)
    late = -(-3 * pairs_here // 8)
    early = pairs_here - late
    sizes = [1, (early - 1) // 2, early - 1 - (early - 1) // 2, late - late // 3, late // 3]
    sizes = [n for n in sizes if n]
    firsts = [sum(sizes[:i]) for i in range(len(sizes))]
    chunks = range(len(sizes))
    split = firsts.index(early)
    shifts = range(1, peers)
    cols = ((place + jnp.arange(peers)) % peers * pairs_here).astype(jnp.int32)
    src = ((place - jnp.arange(peers)) % peers).astype(jnp.int32)

    def move(values):
        return [
            lax.ppermute(value, "head", [(i, (i + s) % peers) for i in range(peers)])
            for s, value in zip(shifts, values)
        ]

    (packed,) = pack(cols, peers, arrays, 0, sizes[:1])
    got = [move(packed)]
    late_sums, *late_sent = source_states(cols, peers, arrays, early, late)
    late_got = move(late_sent)
    for c, packed in zip(chunks[1:], pack(cols, peers, arrays, sizes[0], sizes[1:])):
        got.append(move(packed))
    for piece in late_got:
        late_sums = late_sums + piece.astype(F32)
    sums = []
    for c in chunks[:split]:
        own = states(cols, arrays, got[c], firsts[c], sizes[c])
        if c == 0:
            own = jnp.concatenate([own, late_sums.astype(BF16)], axis=1)
        sums.append(scan(own))

    outs = None
    for c in [*chunks[: split - 1], split, split - 1, *chunks[split + 1 :]]:
        at = 0 if c < split else sizes[0] + firsts[c] - early
        outs = outputs(
            cols, src, arrays, got[c], sums[c if c < split else 0], at, firsts[c], sizes[c], heads_here, scale, outs
        )
    return tuple(outs)


def solution(mesh):
    tokens = P(("seq", "head"), None)
    return jax.shard_map(
        local,
        mesh=mesh,
        in_specs=(tokens,) * 4,
        out_specs=(P("seq", "head"),) * 3,
        check_vma=False,
    )
```

```python
import functools
import math

import jax
import jax.numpy as jnp
from jax import lax
from jax.experimental import pallas as pl
from jax.experimental.pallas import tpu as pltpu
from jax.sharding import PartitionSpec as P


DK = 128
F32 = jnp.float32
BF16 = jnp.bfloat16
PAIR = 2 * DK
VMEM_LIMIT = 67_000_000


NT = (((1,), (1,)), ((), ()))
TN = (((0,), (0,)), ((), ()))
NN = (((1,), (0,)), ((), ()))


def mm(a, b, dims):
    return lax.dot_general(a, b, dims, preferred_element_type=F32)


def cost(flops, size):
    return pl.CostEstimate(flops=flops, bytes_accessed=size, transcendentals=0)


def pack_kernel(sizes, first, peers, cols_ref, *refs):
    count = len(sizes) * (peers - 1)
    ins, outs, bufs = refs[:4], refs[4 : 4 + count], refs[4 + count : 4 + 2 * count]
    in_sem, out_sem = refs[4 + 2 * count :]
    reads, writes = [], []
    for c, n in enumerate(sizes):
        for s in range(peers - 1):
            i = c * (peers - 1) + s
            at = pl.multiple_of((cols_ref[s + 1] + (first + sum(sizes[:c]))) * PAIR, PAIR)
            for j in range(4):
                k = 4 * i + j
                reads.append(
                    pltpu.make_async_copy(ins[j].at[:, pl.ds(at, n * PAIR)], bufs[i].at[j], in_sem.at[k])
                )
                writes.append(pltpu.make_async_copy(bufs[i].at[j], outs[i].at[j], out_sem.at[k]))
    for read in reads:
        read.start()
    for read, write in zip(reads, writes):
        read.wait()
        write.start()
    for write in writes:
        write.wait()


def pack(cols, peers, arrays, first, sizes):
    rows = arrays[0].shape[0]
    shapes = [(4, rows, n * PAIR) for n in sizes for _ in range(1, peers)]
    flat = pl.pallas_call(
        functools.partial(pack_kernel, sizes, first, peers),
        in_specs=[pl.BlockSpec(memory_space=pltpu.SMEM)] + [pl.BlockSpec(memory_space=pl.ANY)] * 4,
        out_specs=[pl.BlockSpec(memory_space=pl.ANY)] * len(shapes),
        out_shape=[jax.ShapeDtypeStruct(shape, BF16) for shape in shapes],
        scratch_shapes=[pltpu.VMEM(shape, BF16) for shape in shapes]
        + [pltpu.SemaphoreType.DMA((4 * len(shapes),))] * 2,
        cost_estimate=cost(0, 16 * rows * sum(sizes) * PAIR * (peers - 1)),
        name="pack",
    )(cols, *arrays)
    return [flat[i * (peers - 1) : (i + 1) * (peers - 1)] for i in range(len(sizes))]


def state_kernel(peers, col_ref, q_ref, k_ref, v_ref, g_ref, *rest):
    out_ref = rest[-1]
    for j in range(PAIR // DK):
        at = slice(j * DK, (j + 1) * DK)
        kv = mm(k_ref[:, at], v_ref[:, at], TN)
        qg = mm(q_ref[:, at], g_ref[:, at], TN)
        for r in rest[:peers]:
            kv = kv + mm(r[1, :, at], r[2, :, at], TN)
            qg = qg + mm(r[0, :, at], r[3, :, at], TN)
        out_ref[0, j] = kv.astype(out_ref.dtype)
        out_ref[1, j] = qg.astype(out_ref.dtype)


def states(cols, arrays, got, first, pairs, dtype=BF16, at=0, room=None, base=0, into=None):
    rows = arrays[0].shape[0]
    own = pl.BlockSpec((rows, PAIR), lambda i, c: (0, c[at] + first + i))
    there = pl.BlockSpec((4, rows, PAIR), lambda i, c: (0, 0, i))
    tokens = rows * (1 + len(got))
    per = PAIR // DK
    shared = [] if into is None else [into]
    return pl.pallas_call(
        functools.partial(state_kernel, len(got)),
        grid_spec=pltpu.PrefetchScalarGridSpec(
            num_scalar_prefetch=1,
            grid=(pairs,),
            in_specs=[own] * 4 + [there] * len(got) + [pl.BlockSpec(memory_space=pl.ANY)] * len(shared),
            out_specs=pl.BlockSpec((2, per, DK, DK), lambda i, c: (0, base + i, 0, 0)),
        ),
        out_shape=jax.ShapeDtypeStruct((2, per * (room or pairs), DK, DK), dtype),
        input_output_aliases={5 + len(got): 0} if shared else {},
        cost_estimate=cost(4 * tokens * DK * PAIR * pairs, 8 * tokens * pairs * PAIR),
        compiler_params=pltpu.CompilerParams(vmem_limit_bytes=VMEM_LIMIT),
        name="states",
    )(cols, *arrays, *got, *shared)


def gather_rows(src_ref, owns, got, which, all_ref):
    rows = owns[0].shape[0]
    mine = pl.multiple_of(src_ref[0] * rows, rows)
    for j in which:
        all_ref[j, pl.ds(mine, rows), :] = owns[j][...]
    for p, r in enumerate(got):
        at = pl.multiple_of(src_ref[p + 1] * rows, rows)
        for j in which:
            all_ref[j, pl.ds(at, rows), :] = r[j]


def within(all_ref, at):
    total = all_ref.shape[1]
    half = total // 2
    up, down = slice(0, half), slice(half, total)
    row = lax.broadcasted_iota(jnp.int32, (half, half), 0)
    column = lax.broadcasted_iota(jnp.int32, (half, half), 1)
    lower, upper = row >= column, row <= column

    def tri(x, keep):
        return jnp.where(keep, x, 0.0).astype(BF16)

    q_a, q_b = all_ref[0, up, at], all_ref[0, down, at]
    k_a, k_b = all_ref[1, up, at], all_ref[1, down, at]
    v_a, v_b = all_ref[2, up, at], all_ref[2, down, at]
    g_a, g_b = all_ref[3, up, at], all_ref[3, down, at]
    yield 0, up, mm(tri(mm(g_a, v_a, NT), lower), k_a, NN)
    yield 0, down, mm(mm(g_b, v_a, NT).astype(BF16), k_a, NN) + mm(tri(mm(g_b, v_b, NT), lower), k_b, NN)
    yield 1, up, mm(tri(mm(v_a, g_a, NT), upper), q_a, NN) + mm(mm(v_a, g_b, NT).astype(BF16), q_b, NN)
    yield 1, down, mm(tri(mm(v_b, g_b, NT), upper), q_b, NN)
    yield 2, up, mm(tri(mm(k_a, q_a, NT), upper), g_a, NN) + mm(mm(k_a, q_b, NT).astype(BF16), g_b, NN)
    yield 2, down, mm(tri(mm(k_b, q_b, NT), upper), g_b, NN)


def across(all_ref, sum_ref, j, grad, rows, at):
    if grad == 0:
        return mm(all_ref[3, rows, at], sum_ref[0, j], NT)
    if grad == 1:
        return mm(all_ref[2, rows, at], sum_ref[1, j], NT)
    return mm(all_ref[1, rows, at], sum_ref[1, j], NN)


def whole_kernel(peers, aliased, scale, col_ref, src_ref, *refs):
    owns, got, sum_ref = refs[:4], refs[4 : 4 + peers], refs[4 + peers]
    outs, all_ref = refs[5 + peers + 3 * aliased : -1], refs[-1]
    gather_rows(src_ref, owns, got, range(4), all_ref)
    for j in range(PAIR // DK):
        at = slice(j * DK, (j + 1) * DK)
        for grad, rows, value in within(all_ref, at):
            value = value + across(all_ref, sum_ref, j, grad, rows, at)
            outs[grad][rows, at] = (scale * value).astype(BF16)


def within_kernel(peers, aliased, scale, col_ref, src_ref, *refs):
    owns, got = refs[:4], refs[4 : 4 + peers]
    outs, rows_ref, all_ref = refs[4 + peers + 4 * aliased : -2], refs[-2], refs[-1]
    gather_rows(src_ref, owns, got, range(4), all_ref)
    rows_ref[...] = all_ref[1:]
    for j in range(PAIR // DK):
        at = slice(j * DK, (j + 1) * DK)
        for grad, rows, value in within(all_ref, at):
            outs[grad][rows, at] = value


def across_kernel(aliased, scale, rows_ref, sum_ref, *refs):
    parts, outs = refs[:3], refs[3 + 3 * aliased :]
    for j in range(PAIR // DK):
        at = slice(j * DK, (j + 1) * DK)
        for grad, (which, state, dims) in enumerate(((2, 0, NT), (1, 1, NT), (0, 1, NN))):
            value = parts[grad][:, at] + mm(rows_ref[which, :, at], sum_ref[state, j], dims)
            outs[grad][:, at] = (scale * value).astype(BF16)


ANY = pl.BlockSpec(memory_space=pl.ANY)


def outputs(kernel, cols, src, arrays, got, sums, first, pairs, base, room, scale, into):
    rows = arrays[0].shape[0]
    total = rows * (1 + len(got))
    whole = kernel is whole_kernel
    own = pl.BlockSpec((rows, PAIR), lambda i, c, s: (0, c[0] + first + i))
    there = pl.BlockSpec((4, rows, PAIR), lambda i, c, s: (0, 0, i))
    operands, specs = [*arrays, *got], [own] * 4 + [there] * len(got)
    here = pl.BlockSpec((total, PAIR), lambda i, c, s: (0, base + i))
    outs, shapes = [here] * 3, [jax.ShapeDtypeStruct((total, room * PAIR), BF16 if whole else F32)] * 3
    if whole:
        sums, offset = sums
        operands.append(sums)
        specs.append(pl.BlockSpec((2, PAIR // DK, DK, DK), lambda i, c, s: (0, offset + i, 0, 0)))
    else:
        outs.append(pl.BlockSpec((3, total, PAIR), lambda i, c, s: (0, 0, base + i)))
        shapes.append(jax.ShapeDtypeStruct((3, total, room * PAIR), BF16))
    start = 2 + len(operands)
    shared = [] if into is None else list(into)
    return pl.pallas_call(
        functools.partial(kernel, len(got), int(into is not None), scale),
        grid_spec=pltpu.PrefetchScalarGridSpec(
            num_scalar_prefetch=2,
            grid=(pairs,),
            in_specs=specs + [ANY] * len(shared),
            out_specs=outs,
            scratch_shapes=[pltpu.VMEM((4, total, PAIR), BF16)],
        ),
        out_shape=shapes,
        input_output_aliases={start + j: j for j in range(len(shared))},
        cost_estimate=cost(14 * total * total * PAIR * pairs, 14 * total * PAIR * pairs),
        compiler_params=pltpu.CompilerParams(vmem_limit_bytes=VMEM_LIMIT),
    )(cols, src, *operands, *shared)


def finish(parts, sums, pairs, room, scale, into):
    total = parts[0].shape[0]
    here = pl.BlockSpec((total, PAIR), lambda i: (0, i))
    shared = [] if into is None else list(into)
    return pl.pallas_call(
        functools.partial(across_kernel, int(into is not None), scale),
        grid=(pairs,),
        in_specs=[
            pl.BlockSpec((3, total, PAIR), lambda i: (0, 0, i)),
            pl.BlockSpec((2, PAIR // DK, DK, DK), lambda i: (0, i, 0, 0)),
            *[here] * 3,
            *[ANY] * len(shared),
        ],
        out_specs=[here] * 3,
        out_shape=[jax.ShapeDtypeStruct((total, room * PAIR), BF16)] * 3,
        input_output_aliases={5 + j: j for j in range(len(shared))},
        cost_estimate=cost(6 * total * DK * PAIR * pairs, 24 * total * PAIR * pairs),
        compiler_params=pltpu.CompilerParams(vmem_limit_bytes=VMEM_LIMIT),
        name="across",
    )(parts[3], sums, *parts[:3], *shared)


def running_kernel(up_ref, part_ref, out_ref):
    count = part_ref.shape[0]

    def run(order):
        total = jnp.zeros(part_ref.shape[1:], F32)
        for i in order:
            out_ref[i] = total.astype(BF16)
            total = total + part_ref[i].astype(F32)

    @pl.when(up_ref[0] == 1)
    def _():
        run(range(count))

    @pl.when(up_ref[0] == 0)
    def _():
        run(reversed(range(count)))


def scan(own):
    count = lax.axis_size("seq")
    part = own.reshape(count, -1, DK)
    parts = lax.all_to_all(part, "seq", 0, 0, tiled=True)
    up = (lax.axis_index("seq") < count // 2).astype(jnp.int32).reshape(1)
    mine = pl.pallas_call(
        running_kernel,
        in_specs=[pl.BlockSpec(memory_space=pltpu.SMEM), pl.BlockSpec(memory_space=pltpu.VMEM)],
        out_specs=pl.BlockSpec(memory_space=pltpu.VMEM),
        out_shape=jax.ShapeDtypeStruct(parts.shape, BF16),
        cost_estimate=cost(parts.size, 4 * parts.size),
        name="running",
    )(up, parts)
    return lax.all_to_all(mine, "seq", 0, 0, tiled=True).reshape(own.shape)


def local(queries, key_vectors, value_vectors, out_grads):
    return grads((queries, key_vectors, value_vectors, out_grads))


def grads(arrays):
    peers = lax.axis_size("head")
    place = lax.axis_index("head")
    rows = arrays[0].shape[0]
    pairs_here = arrays[0].shape[1] // PAIR // peers
    total_tokens = rows * peers * lax.axis_size("seq")
    scale = 1.0 / math.sqrt(DK * total_tokens)
    late = pairs_here // 2
    early = pairs_here - late
    sizes = [early - early // 2, early // 2]
    split = len(sizes)
    sizes += [n for n in (late - 2 * (late // 4), late // 4, late // 4) if n]
    firsts = [sum(sizes[:i]) for i in range(len(sizes))]
    shifts = range(1, peers)
    cols = ((place + jnp.arange(peers)) % peers * pairs_here).astype(jnp.int32)
    src = ((place - jnp.arange(peers)) % peers).astype(jnp.int32)

    def move(values):
        return [
            lax.ppermute(value, "head", [(i, (i + s) % peers) for i in range(peers)])
            for s, value in zip(shifts, values)
        ]

    late_sent = [states(cols, arrays, [], early, late, BF16, s) for s in shifts]
    late_got = move(late_sent)
    got = []
    for packed in pack(cols, peers, arrays, 0, sizes):
        got.append(move(packed))
    late_sums = states(cols, arrays, [], early, late, F32)
    for piece in late_got:
        late_sums = late_sums + piece.astype(F32)
    late_sums = scan(late_sums.astype(BF16))
    early_sums = parts = None
    for c in range(split):
        early_sums = states(
            cols, arrays, got[c], firsts[c], sizes[c], room=early, base=firsts[c], into=early_sums
        )
    for c in range(split):
        parts = outputs(
            within_kernel, cols, src, arrays, got[c], None, firsts[c], sizes[c], firsts[c], early, scale, parts
        )
    early_sums = scan(early_sums)

    outs = None
    for c in range(split, len(sizes)):
        if c == len(sizes) - 1:
            outs = finish(parts, early_sums, early, pairs_here, scale, outs)
        sums = (late_sums, firsts[c] - early)
        outs = outputs(
            whole_kernel, cols, src, arrays, got[c], sums, firsts[c], sizes[c], firsts[c], pairs_here, scale, outs
        )
    return tuple(outs)


def solution(mesh):
    tokens = P(("seq", "head"), None)
    return jax.shard_map(
        local,
        mesh=mesh,
        in_specs=(tokens,) * 4,
        out_specs=(P("seq", "head"),) * 3,
        check_vma=False,
    )
```

```python
import functools
import math

import jax
import jax.numpy as jnp
from jax import lax
from jax.experimental import pallas as pl
from jax.experimental.pallas import tpu as pltpu
from jax.sharding import PartitionSpec as P


DK = 128
F32 = jnp.float32
BF16 = jnp.bfloat16
PAIR = 2 * DK
VMEM_LIMIT = 67_000_000


NT = (((1,), (1,)), ((), ()))
TN = (((0,), (0,)), ((), ()))
NN = (((1,), (0,)), ((), ()))


def mm(a, b, dims):
    return lax.dot_general(a, b, dims, preferred_element_type=F32)


def cost(flops, size):
    return pl.CostEstimate(flops=flops, bytes_accessed=size, transcendentals=0)


def pack_kernel(sizes, first, peers, *refs):
    cols, refs = refs[: peers - 1], refs[peers - 1 :]
    count = len(sizes) * (peers - 1)
    ins, outs, bufs = refs[:4], refs[4 : 4 + count], refs[4 + count : 4 + 2 * count]
    in_sem, out_sem = refs[4 + 2 * count :]
    reads, writes = [], []
    for c, n in enumerate(sizes):
        for s in range(peers - 1):
            i = c * (peers - 1) + s
            at = pl.multiple_of((cols[s][0] + (first + sum(sizes[:c]))) * PAIR, PAIR)
            for j in range(4):
                k = 4 * i + j
                reads.append(
                    pltpu.make_async_copy(ins[j].at[:, pl.ds(at, n * PAIR)], bufs[i].at[j], in_sem.at[k])
                )
                writes.append(pltpu.make_async_copy(bufs[i].at[j], outs[i].at[j], out_sem.at[k]))
    for read in reads:
        read.start()
    for read, write in zip(reads, writes):
        read.wait()
        write.start()
    for write in writes:
        write.wait()


def pack(cols, peers, arrays, first, sizes):
    rows = arrays[0].shape[0]
    shapes = [(4, rows, n * PAIR) for n in sizes for _ in range(1, peers)]
    flat = pl.pallas_call(
        functools.partial(pack_kernel, sizes, first, peers),
        in_specs=[pl.BlockSpec(memory_space=pltpu.SMEM)] * (peers - 1) + [pl.BlockSpec(memory_space=pl.ANY)] * 4,
        out_specs=[pl.BlockSpec(memory_space=pl.ANY)] * len(shapes),
        out_shape=[jax.ShapeDtypeStruct(shape, BF16) for shape in shapes],
        scratch_shapes=[pltpu.VMEM(shape, BF16) for shape in shapes]
        + [pltpu.SemaphoreType.DMA((4 * len(shapes),))] * 2,
        cost_estimate=cost(0, 16 * rows * sum(sizes) * PAIR * (peers - 1)),
        name="pack",
    )(*cols[1:], *arrays)
    return [flat[i * (peers - 1) : (i + 1) * (peers - 1)] for i in range(len(sizes))]


def state_kernel(peers, col_ref, q_ref, k_ref, v_ref, g_ref, *rest):
    out_ref = rest[-1]
    for j in range(PAIR // DK):
        at = slice(j * DK, (j + 1) * DK)
        kv = mm(k_ref[:, at], v_ref[:, at], TN)
        qg = mm(q_ref[:, at], g_ref[:, at], TN)
        for r in rest[:peers]:
            kv = kv + mm(r[1, :, at], r[2, :, at], TN)
            qg = qg + mm(r[0, :, at], r[3, :, at], TN)
        out_ref[0, j] = kv.astype(out_ref.dtype)
        out_ref[1, j] = qg.astype(out_ref.dtype)


def states(cols, arrays, got, first, pairs, dtype=BF16, at=0, room=None, base=0, into=None):
    rows = arrays[0].shape[0]
    own = pl.BlockSpec((rows, PAIR), lambda i, c: (0, c[0] + first + i))
    there = pl.BlockSpec((4, rows, PAIR), lambda i, c: (0, 0, i))
    tokens = rows * (1 + len(got))
    per = PAIR // DK
    shared = [] if into is None else [into]
    return pl.pallas_call(
        functools.partial(state_kernel, len(got)),
        grid_spec=pltpu.PrefetchScalarGridSpec(
            num_scalar_prefetch=1,
            grid=(pairs,),
            in_specs=[own] * 4 + [there] * len(got) + [pl.BlockSpec(memory_space=pl.ANY)] * len(shared),
            out_specs=pl.BlockSpec((2, per, DK, DK), lambda i, c: (0, base + i, 0, 0)),
        ),
        out_shape=jax.ShapeDtypeStruct((2, per * (room or pairs), DK, DK), dtype),
        input_output_aliases={5 + len(got): 0} if shared else {},
        cost_estimate=cost(4 * tokens * DK * PAIR * pairs, 8 * tokens * pairs * PAIR),
        compiler_params=pltpu.CompilerParams(vmem_limit_bytes=VMEM_LIMIT),
        name="states",
    )(cols[at], *arrays, *got, *shared)


def gather_rows(src, owns, got, which, all_ref):
    rows = owns[0].shape[0]
    mine = pl.multiple_of(src[0][0] * rows, rows)
    for j in which:
        all_ref[j, pl.ds(mine, rows), :] = owns[j][...]
    for p, r in enumerate(got):
        at = pl.multiple_of(src[p + 1][0] * rows, rows)
        for j in which:
            all_ref[j, pl.ds(at, rows), :] = r[j]


def within(all_ref, at):
    total = all_ref.shape[1]
    half = total // 2
    up, down = slice(0, half), slice(half, total)
    row = lax.broadcasted_iota(jnp.int32, (half, half), 0)
    column = lax.broadcasted_iota(jnp.int32, (half, half), 1)
    lower, upper = row >= column, row <= column

    def tri(x, keep):
        return jnp.where(keep, x, 0.0).astype(BF16)

    q, k, v, g = (all_ref[j, :, at] for j in range(4))
    probe = mm(g, v[up], NT)
    probe = jnp.concatenate([tri(probe[up], lower), probe[down].astype(BF16)], 0)
    first = mm(probe, k[up], NN)
    second = mm(tri(mm(g[down], v[down], NT), lower), k[down], NN)
    yield 0, up, first[up]
    yield 0, down, first[down] + second
    for grad, left, right in ((1, v, g), (2, k, q)):
        other = q if grad == 1 else g
        late = mm(left, right[down], NT)
        late = jnp.concatenate([late[up].astype(BF16), tri(late[down], upper)], 0)
        second = mm(late, other[down], NN)
        first = mm(tri(mm(left[up], right[up], NT), upper), other[up], NN)
        yield grad, up, first + second[up]
        yield grad, down, second[down]


def across(all_ref, sum_ref, j, grad, rows, at):
    if grad == 0:
        return mm(all_ref[3, rows, at], sum_ref[0, j], NT)
    if grad == 1:
        return mm(all_ref[2, rows, at], sum_ref[1, j], NT)
    return mm(all_ref[1, rows, at], sum_ref[1, j], NN)


def whole_kernel(peers, aliased, scale, col_ref, *refs):
    src, refs = refs[: peers + 1], refs[peers + 1 :]
    owns, got, sum_ref = refs[:4], refs[4 : 4 + peers], refs[4 + peers]
    outs, all_ref = refs[5 + peers + 3 * aliased : -1], refs[-1]
    gather_rows(src, owns, got, range(4), all_ref)
    for j in range(PAIR // DK):
        at = slice(j * DK, (j + 1) * DK)
        for grad, rows, value in within(all_ref, at):
            value = value + across(all_ref, sum_ref, j, grad, rows, at)
            outs[grad][rows, at] = (scale * value).astype(BF16)


def within_kernel(peers, aliased, scale, col_ref, *refs):
    src, refs = refs[: peers + 1], refs[peers + 1 :]
    owns, got = refs[:4], refs[4 : 4 + peers]
    outs, rows_ref, all_ref = refs[4 + peers + 4 * aliased : -2], refs[-2], refs[-1]
    gather_rows(src, owns, got, range(4), all_ref)
    rows_ref[...] = all_ref[1:]
    for j in range(PAIR // DK):
        at = slice(j * DK, (j + 1) * DK)
        for grad, rows, value in within(all_ref, at):
            outs[grad][rows, at] = value


def across_kernel(aliased, scale, rows_ref, sum_ref, *refs):
    parts, outs = refs[:3], refs[3 + 3 * aliased :]
    for j in range(PAIR // DK):
        at = slice(j * DK, (j + 1) * DK)
        for grad, (which, state, dims) in enumerate(((2, 0, NT), (1, 1, NT), (0, 1, NN))):
            value = parts[grad][:, at] + mm(rows_ref[which, :, at], sum_ref[state, j], dims)
            outs[grad][:, at] = (scale * value).astype(BF16)


ANY = pl.BlockSpec(memory_space=pl.ANY)


def outputs(kernel, cols, src, arrays, got, sums, first, pairs, base, room, scale, into):
    rows = arrays[0].shape[0]
    total = rows * (1 + len(got))
    whole = kernel is whole_kernel
    own = pl.BlockSpec((rows, PAIR), lambda i, c, *s: (0, c[0] + first + i))
    there = pl.BlockSpec((4, rows, PAIR), lambda i, c, *s: (0, 0, i))
    operands, specs = [*arrays, *got], [own] * 4 + [there] * len(got)
    here = pl.BlockSpec((total, PAIR), lambda i, c, *s: (0, base + i))
    outs, shapes = [here] * 3, [jax.ShapeDtypeStruct((total, room * PAIR), BF16 if whole else F32)] * 3
    if whole:
        sums, offset = sums
        operands.append(sums)
        specs.append(pl.BlockSpec((2, PAIR // DK, DK, DK), lambda i, c, *s: (0, offset + i, 0, 0)))
    else:
        outs.append(pl.BlockSpec((3, total, PAIR), lambda i, c, *s: (0, 0, base + i)))
        shapes.append(jax.ShapeDtypeStruct((3, total, room * PAIR), BF16))
    start = 1 + len(src) + len(operands)
    shared = [] if into is None else list(into)
    return pl.pallas_call(
        functools.partial(kernel, len(got), int(into is not None), scale),
        grid_spec=pltpu.PrefetchScalarGridSpec(
            num_scalar_prefetch=1 + len(src),
            grid=(pairs,),
            in_specs=specs + [ANY] * len(shared),
            out_specs=outs,
            scratch_shapes=[pltpu.VMEM((4, total, PAIR), BF16)],
        ),
        out_shape=shapes,
        input_output_aliases={start + j: j for j in range(len(shared))},
        cost_estimate=cost(14 * total * total * PAIR * pairs, 14 * total * PAIR * pairs),
        compiler_params=pltpu.CompilerParams(vmem_limit_bytes=VMEM_LIMIT),
    )(cols[0], *src, *operands, *shared)


def finish(parts, sums, pairs, room, scale, into):
    total = parts[0].shape[0]
    here = pl.BlockSpec((total, PAIR), lambda i: (0, i))
    shared = [] if into is None else list(into)
    return pl.pallas_call(
        functools.partial(across_kernel, int(into is not None), scale),
        grid=(pairs,),
        in_specs=[
            pl.BlockSpec((3, total, PAIR), lambda i: (0, 0, i)),
            pl.BlockSpec((2, PAIR // DK, DK, DK), lambda i: (0, i, 0, 0)),
            *[here] * 3,
            *[ANY] * len(shared),
        ],
        out_specs=[here] * 3,
        out_shape=[jax.ShapeDtypeStruct((total, room * PAIR), BF16)] * 3,
        input_output_aliases={5 + j: j for j in range(len(shared))},
        cost_estimate=cost(6 * total * DK * PAIR * pairs, 24 * total * PAIR * pairs),
        compiler_params=pltpu.CompilerParams(vmem_limit_bytes=VMEM_LIMIT),
        name="across",
    )(parts[3], sums, *parts[:3], *shared)


def running_kernel(up_ref, part_ref, out_ref):
    count = part_ref.shape[0]

    def run(order):
        total = jnp.zeros(part_ref.shape[1:], F32)
        for i in order:
            out_ref[i] = total.astype(BF16)
            total = total + part_ref[i].astype(F32)

    @pl.when(up_ref[0] == 1)
    def _():
        run(range(count))

    @pl.when(up_ref[0] == 0)
    def _():
        run(reversed(range(count)))


def scan(own):
    count = lax.axis_size("seq")
    part = own.reshape(count, -1, DK)
    parts = lax.all_to_all(part, "seq", 0, 0, tiled=True)
    up = (lax.axis_index("seq") < count // 2).astype(jnp.int32).reshape(1)
    mine = pl.pallas_call(
        running_kernel,
        in_specs=[pl.BlockSpec(memory_space=pltpu.SMEM), pl.BlockSpec(memory_space=pltpu.VMEM)],
        out_specs=pl.BlockSpec(memory_space=pltpu.VMEM),
        out_shape=jax.ShapeDtypeStruct(parts.shape, BF16),
        cost_estimate=cost(parts.size, 4 * parts.size),
        name="running",
    )(up, parts)
    return lax.all_to_all(mine, "seq", 0, 0, tiled=True).reshape(own.shape)


def local(queries, key_vectors, value_vectors, out_grads):
    return grads((queries, key_vectors, value_vectors, out_grads))


def grads(arrays):
    peers = lax.axis_size("head")
    place = lax.axis_index("head")
    rows = arrays[0].shape[0]
    pairs_here = arrays[0].shape[1] // PAIR // peers
    total_tokens = rows * peers * lax.axis_size("seq")
    scale = 1.0 / math.sqrt(DK * total_tokens)
    late = pairs_here // 2
    early = pairs_here - late
    sizes = [early - early // 2, early // 2]
    split = len(sizes)
    sizes += [n for n in (late - 2 * (late // 4), late // 4, late // 4) if n]
    firsts = [sum(sizes[:i]) for i in range(len(sizes))]
    shifts = range(1, peers)
    cols = [jnp.reshape((place + s) % peers * pairs_here, (1,)).astype(jnp.int32) for s in range(peers)]
    src = [jnp.reshape((place - s) % peers, (1,)).astype(jnp.int32) for s in range(peers)]

    def move(values):
        return [
            lax.ppermute(value, "head", [(i, (i + s) % peers) for i in range(peers)])
            for s, value in zip(shifts, values)
        ]

    late_sent = [states(cols, arrays, [], early, late, BF16, s) for s in shifts]
    late_got = move(late_sent)
    got = []
    for packed in pack(cols, peers, arrays, 0, sizes):
        got.append(move(packed))
    late_sums = states(cols, arrays, [], early, late, F32)
    for piece in late_got:
        late_sums = late_sums + piece.astype(F32)
    late_sums = scan(late_sums.astype(BF16))
    early_sums = parts = None
    for c in range(split):
        early_sums = states(
            cols, arrays, got[c], firsts[c], sizes[c], room=early, base=firsts[c], into=early_sums
        )
    for c in range(split):
        parts = outputs(
            within_kernel, cols, src, arrays, got[c], None, firsts[c], sizes[c], firsts[c], early, scale, parts
        )
    early_sums = scan(early_sums)

    outs = None
    for c in range(split, len(sizes)):
        if c == len(sizes) - 1:
            outs = finish(parts, early_sums, early, pairs_here, scale, outs)
        sums = (late_sums, firsts[c] - early)
        outs = outputs(
            whole_kernel, cols, src, arrays, got[c], sums, firsts[c], sizes[c], firsts[c], pairs_here, scale, outs
        )
    return tuple(outs)


def solution(mesh):
    tokens = P(("seq", "head"), None)
    return jax.shard_map(
        local,
        mesh=mesh,
        in_specs=(tokens,) * 4,
        out_specs=(P("seq", "head"),) * 3,
        check_vma=False,
    )
```

```python
import functools
import math

import jax
import jax.numpy as jnp
from jax import lax
from jax.experimental import pallas as pl
from jax.experimental.pallas import tpu as pltpu
from jax.sharding import PartitionSpec as P


DK = 128
F32 = jnp.float32
BF16 = jnp.bfloat16
PAIR = 2 * DK
VMEM_LIMIT = 67_000_000


NT = (((1,), (1,)), ((), ()))
TN = (((0,), (0,)), ((), ()))
NN = (((1,), (0,)), ((), ()))


def mm(a, b, dims):
    return lax.dot_general(a, b, dims, preferred_element_type=F32)


def cost(flops, size):
    return pl.CostEstimate(flops=flops, bytes_accessed=size, transcendentals=0)


def pack_kernel(sizes, first, peers, *refs):
    cols, refs = refs[: peers - 1], refs[peers - 1 :]
    count = len(sizes) * (peers - 1)
    ins, outs, bufs = refs[:4], refs[4 : 4 + count], refs[4 + count : 4 + 2 * count]
    in_sem, out_sem = refs[4 + 2 * count :]
    reads, writes = [], []
    for c, n in enumerate(sizes):
        for s in range(peers - 1):
            i = c * (peers - 1) + s
            at = pl.multiple_of((cols[s][0] + (first + sum(sizes[:c]))) * PAIR, PAIR)
            for j in range(4):
                k = 4 * i + j
                reads.append(
                    pltpu.make_async_copy(ins[j].at[:, pl.ds(at, n * PAIR)], bufs[i].at[j], in_sem.at[k])
                )
                writes.append(pltpu.make_async_copy(bufs[i].at[j], outs[i].at[j], out_sem.at[k]))
    for read in reads:
        read.start()
    for read, write in zip(reads, writes):
        read.wait()
        write.start()
    for write in writes:
        write.wait()


def pack(cols, peers, arrays, first, sizes):
    rows = arrays[0].shape[0]
    shapes = [(4, rows, n * PAIR) for n in sizes for _ in range(1, peers)]
    flat = pl.pallas_call(
        functools.partial(pack_kernel, sizes, first, peers),
        in_specs=[pl.BlockSpec(memory_space=pltpu.SMEM)] * (peers - 1) + [pl.BlockSpec(memory_space=pl.ANY)] * 4,
        out_specs=[pl.BlockSpec(memory_space=pl.ANY)] * len(shapes),
        out_shape=[jax.ShapeDtypeStruct(shape, BF16) for shape in shapes],
        scratch_shapes=[pltpu.VMEM(shape, BF16) for shape in shapes]
        + [pltpu.SemaphoreType.DMA((4 * len(shapes),))] * 2,
        cost_estimate=cost(0, 16 * rows * sum(sizes) * PAIR * (peers - 1)),
        name="pack",
    )(*cols[1:], *arrays)
    return [flat[i * (peers - 1) : (i + 1) * (peers - 1)] for i in range(len(sizes))]


def state_kernel(peers, col_ref, q_ref, k_ref, v_ref, g_ref, *rest):
    out_ref = rest[-1]
    for j in range(PAIR // DK):
        at = slice(j * DK, (j + 1) * DK)
        kv = mm(k_ref[:, at], v_ref[:, at], TN)
        qg = mm(q_ref[:, at], g_ref[:, at], TN)
        for r in rest[:peers]:
            kv = kv + mm(r[1, :, at], r[2, :, at], TN)
            qg = qg + mm(r[0, :, at], r[3, :, at], TN)
        out_ref[0, j] = kv.astype(out_ref.dtype)
        out_ref[1, j] = qg.astype(out_ref.dtype)


def states(cols, arrays, got, first, pairs, dtype=BF16, at=0, room=None, base=0, into=None):
    rows = arrays[0].shape[0]
    own = pl.BlockSpec((rows, PAIR), lambda i, c: (0, c[0] + first + i))
    there = pl.BlockSpec((4, rows, PAIR), lambda i, c: (0, 0, i))
    tokens = rows * (1 + len(got))
    per = PAIR // DK
    shared = [] if into is None else [into]
    return pl.pallas_call(
        functools.partial(state_kernel, len(got)),
        grid_spec=pltpu.PrefetchScalarGridSpec(
            num_scalar_prefetch=1,
            grid=(pairs,),
            in_specs=[own] * 4 + [there] * len(got) + [pl.BlockSpec(memory_space=pl.ANY)] * len(shared),
            out_specs=pl.BlockSpec((2, per, DK, DK), lambda i, c: (0, base + i, 0, 0)),
        ),
        out_shape=jax.ShapeDtypeStruct((2, per * (room or pairs), DK, DK), dtype),
        input_output_aliases={5 + len(got): 0} if shared else {},
        cost_estimate=cost(4 * tokens * DK * PAIR * pairs, 8 * tokens * pairs * PAIR),
        compiler_params=pltpu.CompilerParams(vmem_limit_bytes=VMEM_LIMIT),
        name="states",
    )(cols[at], *arrays, *got, *shared)


def split_kernel(peers, col_ref, core_ref, q_ref, k_ref, v_ref, g_ref, *rest):
    keep_ref, give_ref = rest[-2:]
    first = core_ref[0] == 0
    for j in range(PAIR // DK):
        at = slice(j * DK, (j + 1) * DK)
        kv = mm(k_ref[:, at], v_ref[:, at], TN)
        qg = mm(q_ref[:, at], g_ref[:, at], TN)
        for r in rest[:peers]:
            kv = kv + mm(r[1, :, at], r[2, :, at], TN)
            qg = qg + mm(r[0, :, at], r[3, :, at], TN)
        keep_ref[j] = jnp.where(first, kv, qg)
        give_ref[j] = jnp.where(first, qg, kv)


def split_states(cols, core, arrays, got, first, pairs, base, room, into):
    rows = arrays[0].shape[0]
    own = pl.BlockSpec((rows, PAIR), lambda i, c, d: (0, c[0] + first + i))
    there = pl.BlockSpec((4, rows, PAIR), lambda i, c, d: (0, 0, i))
    tokens = rows * (1 + len(got))
    per = PAIR // DK
    shared = [] if into is None else list(into)
    return pl.pallas_call(
        functools.partial(split_kernel, len(got)),
        grid_spec=pltpu.PrefetchScalarGridSpec(
            num_scalar_prefetch=2,
            grid=(pairs,),
            in_specs=[own] * 4 + [there] * len(got) + [pl.BlockSpec(memory_space=pl.ANY)] * len(shared),
            out_specs=[pl.BlockSpec((per, DK, DK), lambda i, c, d: (base + i, 0, 0))] * 2,
        ),
        out_shape=[jax.ShapeDtypeStruct((per * room, DK, DK), F32)] * 2,
        input_output_aliases={6 + len(got) + j: j for j in range(len(shared))},
        cost_estimate=cost(4 * tokens * DK * PAIR * pairs, 8 * tokens * pairs * PAIR),
        compiler_params=pltpu.CompilerParams(vmem_limit_bytes=VMEM_LIMIT),
        name="split_states",
    )(cols[0], core, *arrays, *got, *shared)


def gather_rows(src, owns, got, which, all_ref):
    rows = owns[0].shape[0]
    mine = pl.multiple_of(src[0][0] * rows, rows)
    for j in which:
        all_ref[j, pl.ds(mine, rows), :] = owns[j][...]
    for p, r in enumerate(got):
        at = pl.multiple_of(src[p + 1][0] * rows, rows)
        for j in which:
            all_ref[j, pl.ds(at, rows), :] = r[j]


def within(all_ref, at):
    total = all_ref.shape[1]
    half = total // 2
    up, down = slice(0, half), slice(half, total)
    row = lax.broadcasted_iota(jnp.int32, (half, half), 0)
    column = lax.broadcasted_iota(jnp.int32, (half, half), 1)
    lower, upper = row >= column, row <= column

    def tri(x, keep):
        return jnp.where(keep, x, 0.0).astype(BF16)

    q, k, v, g = (all_ref[j, :, at] for j in range(4))
    probe = mm(g, v[up], NT)
    probe = jnp.concatenate([tri(probe[up], lower), probe[down].astype(BF16)], 0)
    first = mm(probe, k[up], NN)
    second = mm(tri(mm(g[down], v[down], NT), lower), k[down], NN)
    yield 0, up, first[up]
    yield 0, down, first[down] + second
    for grad, left, right in ((1, v, g), (2, k, q)):
        other = q if grad == 1 else g
        late = mm(left, right[down], NT)
        late = jnp.concatenate([late[up].astype(BF16), tri(late[down], upper)], 0)
        second = mm(late, other[down], NN)
        first = mm(tri(mm(left[up], right[up], NT), upper), other[up], NN)
        yield grad, up, first + second[up]
        yield grad, down, second[down]


def prefix_suffix(core_ref, mine_ref, other_ref, j):
    first, mine, other = core_ref[0] == 0, mine_ref[j], other_ref[j]
    return jnp.where(first, mine, other), jnp.where(first, other, mine)


def whole_kernel(peers, aliased, scale, col_ref, core_ref, *refs):
    src, refs = refs[: peers + 1], refs[peers + 1 :]
    owns, got, sums = refs[:4], refs[4 : 4 + peers], refs[4 + peers : 6 + peers]
    outs, all_ref = refs[6 + peers + 3 * aliased : -1], refs[-1]
    gather_rows(src, owns, got, range(4), all_ref)
    for j in range(PAIR // DK):
        at = slice(j * DK, (j + 1) * DK)
        prefix, suffix = prefix_suffix(core_ref, *sums, j)
        for grad, rows, value in within(all_ref, at):
            which, state, dims = ((3, prefix, NT), (2, suffix, NT), (1, suffix, NN))[grad]
            value = value + mm(all_ref[which, rows, at], state, dims)
            outs[grad][rows, at] = (scale * value).astype(BF16)


def within_kernel(peers, aliased, scale, col_ref, core_ref, *refs):
    src, refs = refs[: peers + 1], refs[peers + 1 :]
    owns, got = refs[:4], refs[4 : 4 + peers]
    outs, rows_ref, all_ref = refs[4 + peers + 4 * aliased : -2], refs[-2], refs[-1]
    gather_rows(src, owns, got, range(4), all_ref)
    rows_ref[...] = all_ref[1:]
    for j in range(PAIR // DK):
        at = slice(j * DK, (j + 1) * DK)
        for grad, rows, value in within(all_ref, at):
            outs[grad][rows, at] = value


def across_kernel(aliased, scale, core_ref, rows_ref, mine_ref, other_ref, *refs):
    parts, outs = refs[:3], refs[3 + 3 * aliased :]
    for j in range(PAIR // DK):
        at = slice(j * DK, (j + 1) * DK)
        prefix, suffix = prefix_suffix(core_ref, mine_ref, other_ref, j)
        for grad, (which, state, dims) in enumerate(((2, prefix, NT), (1, suffix, NT), (0, suffix, NN))):
            value = parts[grad][:, at] + mm(rows_ref[which, :, at], state, dims)
            outs[grad][:, at] = (scale * value).astype(BF16)


ANY = pl.BlockSpec(memory_space=pl.ANY)


def outputs(kernel, cols, core, src, arrays, got, sums, first, pairs, base, room, scale, into):
    rows = arrays[0].shape[0]
    total = rows * (1 + len(got))
    whole = kernel is whole_kernel
    own = pl.BlockSpec((rows, PAIR), lambda i, c, *s: (0, c[0] + first + i))
    there = pl.BlockSpec((4, rows, PAIR), lambda i, c, *s: (0, 0, i))
    operands, specs = [*arrays, *got], [own] * 4 + [there] * len(got)
    here = pl.BlockSpec((total, PAIR), lambda i, c, *s: (0, base + i))
    outs, shapes = [here] * 3, [jax.ShapeDtypeStruct((total, room * PAIR), BF16 if whole else F32)] * 3
    if whole:
        sums, offset = sums
        operands += sums
        specs += [pl.BlockSpec((PAIR // DK, DK, DK), lambda i, c, *s: (offset + i, 0, 0))] * 2
    else:
        outs.append(pl.BlockSpec((3, total, PAIR), lambda i, c, *s: (0, 0, base + i)))
        shapes.append(jax.ShapeDtypeStruct((3, total, room * PAIR), BF16))
    start = 2 + len(src) + len(operands)
    shared = [] if into is None else list(into)
    return pl.pallas_call(
        functools.partial(kernel, len(got), int(into is not None), scale),
        grid_spec=pltpu.PrefetchScalarGridSpec(
            num_scalar_prefetch=2 + len(src),
            grid=(pairs,),
            in_specs=specs + [ANY] * len(shared),
            out_specs=outs,
            scratch_shapes=[pltpu.VMEM((4, total, PAIR), BF16)],
        ),
        out_shape=shapes,
        input_output_aliases={start + j: j for j in range(len(shared))},
        cost_estimate=cost(14 * total * total * PAIR * pairs, 14 * total * PAIR * pairs),
        compiler_params=pltpu.CompilerParams(vmem_limit_bytes=VMEM_LIMIT),
    )(cols[0], core, *src, *operands, *shared)


def finish(parts, core, sums, pairs, room, scale, into):
    total = parts[0].shape[0]
    here = pl.BlockSpec((total, PAIR), lambda i, d: (0, i))
    shared = [] if into is None else list(into)
    return pl.pallas_call(
        functools.partial(across_kernel, int(into is not None), scale),
        grid_spec=pltpu.PrefetchScalarGridSpec(
            num_scalar_prefetch=1,
            grid=(pairs,),
            in_specs=[
                pl.BlockSpec((3, total, PAIR), lambda i, d: (0, 0, i)),
                *[pl.BlockSpec((PAIR // DK, DK, DK), lambda i, d: (i, 0, 0))] * 2,
                *[here] * 3,
                *[ANY] * len(shared),
            ],
            out_specs=[here] * 3,
        ),
        out_shape=[jax.ShapeDtypeStruct((total, room * PAIR), BF16)] * 3,
        input_output_aliases={7 + j: j for j in range(len(shared))},
        cost_estimate=cost(6 * total * DK * PAIR * pairs, 24 * total * PAIR * pairs),
        compiler_params=pltpu.CompilerParams(vmem_limit_bytes=VMEM_LIMIT),
        name="across",
    )(core, parts[3], *sums, *parts[:3], *shared)


def running_kernel(up_ref, part_ref, out_ref):
    count = part_ref.shape[0]

    def run(order):
        total = jnp.zeros(part_ref.shape[1:], F32)
        for i in order:
            out_ref[i] = total.astype(BF16)
            total = total + part_ref[i].astype(F32)

    @pl.when(up_ref[0] == 1)
    def _():
        run(range(count))

    @pl.when(up_ref[0] == 0)
    def _():
        run(reversed(range(count)))


def deal_and_sum(own, up, groups):
    count = len(groups[0])
    parts = lax.all_to_all(own.reshape(count, -1, DK), "seq", 0, 0, tiled=True, axis_index_groups=groups)
    mine = pl.pallas_call(
        running_kernel,
        in_specs=[pl.BlockSpec(memory_space=pltpu.SMEM), pl.BlockSpec(memory_space=pltpu.VMEM)],
        out_specs=pl.BlockSpec(memory_space=pltpu.VMEM),
        out_shape=jax.ShapeDtypeStruct(parts.shape, BF16),
        cost_estimate=cost(parts.size, 4 * parts.size),
        name="running",
    )(up.astype(jnp.int32).reshape(1), parts)
    mine = lax.all_to_all(mine, "seq", 0, 0, tiled=True, axis_index_groups=groups)
    return mine.reshape(own.shape)


def scan_chips(keep, give):
    count = lax.axis_size("seq")
    swap = [(i, i ^ 1) for i in range(count)]
    chip = keep + lax.ppermute(give, "seq", swap)
    groups = [list(range(core, count, 2)) for core in (0, 1)]
    mine = deal_and_sum(chip.astype(BF16), lax.axis_index("seq") % 2 == 0, groups)
    return mine, lax.ppermute((mine.astype(F32) + keep).astype(BF16), "seq", swap)


def local(queries, key_vectors, value_vectors, out_grads):
    return grads((queries, key_vectors, value_vectors, out_grads))


def grads(arrays):
    peers = lax.axis_size("head")
    place = lax.axis_index("head")
    rows = arrays[0].shape[0]
    pairs_here = arrays[0].shape[1] // PAIR // peers
    total_tokens = rows * peers * lax.axis_size("seq")
    scale = 1.0 / math.sqrt(DK * total_tokens)
    late = pairs_here // 2
    early = pairs_here - late
    sizes = [n for n in (1, (early - 1) // 2, early - 1 - (early - 1) // 2) if n]
    split = len(sizes)
    sizes += [n for n in (late - 2 * (late // 4), late // 4, late // 4) if n]
    firsts = [sum(sizes[:i]) for i in range(len(sizes))]
    shifts = range(1, peers)
    cols = [jnp.reshape((place + s) % peers * pairs_here, (1,)).astype(jnp.int32) for s in range(peers)]
    src = [jnp.reshape((place - s) % peers, (1,)).astype(jnp.int32) for s in range(peers)]

    def move(values):
        return [
            lax.ppermute(value, "head", [(i, (i + s) % peers) for i in range(peers)])
            for s, value in zip(shifts, values)
        ]

    got = [move(pack(cols, peers, arrays, 0, sizes[:1])[0])]
    late_sent = [states(cols, arrays, [], early, late, BF16, s) for s in shifts]
    late_got = move(late_sent)
    for c, packed in enumerate(pack(cols, peers, arrays, sizes[0], sizes[1:]), 1):
        got.append(move(packed))
    core = (lax.axis_index("seq") % 2).astype(jnp.int32).reshape(1)
    keep, give = split_states(cols, core, arrays, [], early, late, 0, late, None)
    for piece in late_got:
        first, second = jnp.where(core[0] == 0, piece[0], piece[1]), jnp.where(core[0] == 0, piece[1], piece[0])
        keep, give = keep + first.astype(F32), give + second.astype(F32)
    late_sums = scan_chips(keep, give)
    own = parts = None
    for c in range(split):
        own = split_states(cols, core, arrays, got[c], firsts[c], sizes[c], firsts[c], early, own)
    for c in range(split):
        parts = outputs(
            within_kernel, cols, core, src, arrays, got[c], None, firsts[c], sizes[c], firsts[c], early, scale, parts
        )
    early_sums = scan_chips(*own)

    outs = None
    for c in range(split, len(sizes)):
        if c == len(sizes) - 1:
            outs = finish(parts, core, early_sums, early, pairs_here, scale, outs)
        sums = (late_sums, firsts[c] - early)
        outs = outputs(
            whole_kernel, cols, core, src, arrays, got[c], sums, firsts[c], sizes[c], firsts[c], pairs_here, scale, outs
        )
    return tuple(outs)


def solution(mesh):
    tokens = P(("seq", "head"), None)
    return jax.shard_map(
        local,
        mesh=mesh,
        in_specs=(tokens,) * 4,
        out_specs=(P("seq", "head"),) * 3,
        check_vma=False,
    )
```

```python
import functools
import math

import jax
import jax.numpy as jnp
from jax import lax
from jax.experimental import pallas as pl
from jax.experimental.pallas import tpu as pltpu
from jax.sharding import PartitionSpec as P


DK = 128
F32 = jnp.float32
BF16 = jnp.bfloat16
PAIR = 2 * DK
VMEM_LIMIT = 67_000_000


NT = (((1,), (1,)), ((), ()))
TN = (((0,), (0,)), ((), ()))
NN = (((1,), (0,)), ((), ()))


def mm(a, b, dims):
    return lax.dot_general(a, b, dims, preferred_element_type=F32)


def cost(flops, size):
    return pl.CostEstimate(flops=flops, bytes_accessed=size, transcendentals=0)


def pack_kernel(sizes, first, peers, *refs):
    cols, refs = refs[: peers - 1], refs[peers - 1 :]
    count = len(sizes) * (peers - 1)
    ins, outs, bufs = refs[:4], refs[4 : 4 + count], refs[4 + count : 4 + 2 * count]
    in_sem, out_sem = refs[4 + 2 * count :]
    reads, writes = [], []
    for c, n in enumerate(sizes):
        for s in range(peers - 1):
            i = c * (peers - 1) + s
            at = pl.multiple_of((cols[s][0] + (first + sum(sizes[:c]))) * PAIR, PAIR)
            for j in range(4):
                k = 4 * i + j
                reads.append(
                    pltpu.make_async_copy(ins[j].at[:, pl.ds(at, n * PAIR)], bufs[i].at[j], in_sem.at[k])
                )
                writes.append(pltpu.make_async_copy(bufs[i].at[j], outs[i].at[j], out_sem.at[k]))
    for read in reads:
        read.start()
    for read, write in zip(reads, writes):
        read.wait()
        write.start()
    for write in writes:
        write.wait()


def pack(cols, peers, arrays, first, sizes):
    rows = arrays[0].shape[0]
    shapes = [(4, rows, n * PAIR) for n in sizes for _ in range(1, peers)]
    flat = pl.pallas_call(
        functools.partial(pack_kernel, sizes, first, peers),
        in_specs=[pl.BlockSpec(memory_space=pltpu.SMEM)] * (peers - 1) + [pl.BlockSpec(memory_space=pl.ANY)] * 4,
        out_specs=[pl.BlockSpec(memory_space=pl.ANY)] * len(shapes),
        out_shape=[jax.ShapeDtypeStruct(shape, BF16) for shape in shapes],
        scratch_shapes=[pltpu.VMEM(shape, BF16) for shape in shapes]
        + [pltpu.SemaphoreType.DMA((4 * len(shapes),))] * 2,
        cost_estimate=cost(0, 16 * rows * sum(sizes) * PAIR * (peers - 1)),
        name="pack",
    )(*cols[1:], *arrays)
    return [flat[i * (peers - 1) : (i + 1) * (peers - 1)] for i in range(len(sizes))]


def state_kernel(peers, col_ref, q_ref, k_ref, v_ref, g_ref, *rest):
    out_ref = rest[-1]
    for j in range(PAIR // DK):
        at = slice(j * DK, (j + 1) * DK)
        kv = mm(k_ref[:, at], v_ref[:, at], TN)
        qg = mm(q_ref[:, at], g_ref[:, at], TN)
        for r in rest[:peers]:
            kv = kv + mm(r[1, :, at], r[2, :, at], TN)
            qg = qg + mm(r[0, :, at], r[3, :, at], TN)
        out_ref[0, j] = kv.astype(out_ref.dtype)
        out_ref[1, j] = qg.astype(out_ref.dtype)


def states(cols, arrays, got, first, pairs, dtype=BF16, at=0, room=None, base=0, into=None):
    rows = arrays[0].shape[0]
    own = pl.BlockSpec((rows, PAIR), lambda i, c: (0, c[0] + first + i))
    there = pl.BlockSpec((4, rows, PAIR), lambda i, c: (0, 0, i))
    tokens = rows * (1 + len(got))
    per = PAIR // DK
    shared = [] if into is None else [into]
    return pl.pallas_call(
        functools.partial(state_kernel, len(got)),
        grid_spec=pltpu.PrefetchScalarGridSpec(
            num_scalar_prefetch=1,
            grid=(pairs,),
            in_specs=[own] * 4 + [there] * len(got) + [pl.BlockSpec(memory_space=pl.ANY)] * len(shared),
            out_specs=pl.BlockSpec((2, per, DK, DK), lambda i, c: (0, base + i, 0, 0)),
        ),
        out_shape=jax.ShapeDtypeStruct((2, per * (room or pairs), DK, DK), dtype),
        input_output_aliases={5 + len(got): 0} if shared else {},
        cost_estimate=cost(4 * tokens * DK * PAIR * pairs, 8 * tokens * pairs * PAIR),
        compiler_params=pltpu.CompilerParams(vmem_limit_bytes=VMEM_LIMIT),
        name="states",
    )(cols[at], *arrays, *got, *shared)


def split_kernel(peers, col_ref, core_ref, q_ref, k_ref, v_ref, g_ref, *rest):
    keep_ref, give_ref = rest[-2:]
    first = core_ref[0] == 0
    for j in range(PAIR // DK):
        at = slice(j * DK, (j + 1) * DK)
        kv = mm(k_ref[:, at], v_ref[:, at], TN)
        qg = mm(q_ref[:, at], g_ref[:, at], TN)
        for r in rest[:peers]:
            kv = kv + mm(r[1, :, at], r[2, :, at], TN)
            qg = qg + mm(r[0, :, at], r[3, :, at], TN)
        keep_ref[j] = jnp.where(first, kv, qg)
        give_ref[j] = jnp.where(first, qg, kv)


def split_states(cols, core, arrays, got, first, pairs, base, room, into):
    rows = arrays[0].shape[0]
    own = pl.BlockSpec((rows, PAIR), lambda i, c, d: (0, c[0] + first + i))
    there = pl.BlockSpec((4, rows, PAIR), lambda i, c, d: (0, 0, i))
    tokens = rows * (1 + len(got))
    per = PAIR // DK
    shared = [] if into is None else list(into)
    return pl.pallas_call(
        functools.partial(split_kernel, len(got)),
        grid_spec=pltpu.PrefetchScalarGridSpec(
            num_scalar_prefetch=2,
            grid=(pairs,),
            in_specs=[own] * 4 + [there] * len(got) + [pl.BlockSpec(memory_space=pl.ANY)] * len(shared),
            out_specs=[pl.BlockSpec((per, DK, DK), lambda i, c, d: (base + i, 0, 0))] * 2,
        ),
        out_shape=[jax.ShapeDtypeStruct((per * room, DK, DK), F32)] * 2,
        input_output_aliases={6 + len(got) + j: j for j in range(len(shared))},
        cost_estimate=cost(4 * tokens * DK * PAIR * pairs, 8 * tokens * pairs * PAIR),
        compiler_params=pltpu.CompilerParams(vmem_limit_bytes=VMEM_LIMIT),
        name="split_states",
    )(cols[0], core, *arrays, *got, *shared)


def gather_rows(src, owns, got, which, all_ref):
    rows = owns[0].shape[0]
    mine = pl.multiple_of(src[0][0] * rows, rows)
    for j in which:
        all_ref[j, pl.ds(mine, rows), :] = owns[j][...]
    for p, r in enumerate(got):
        at = pl.multiple_of(src[p + 1][0] * rows, rows)
        for j in which:
            all_ref[j, pl.ds(at, rows), :] = r[j]


def within(all_ref, at):
    total = all_ref.shape[1]
    half = total // 2
    up, down = slice(0, half), slice(half, total)
    row = lax.broadcasted_iota(jnp.int32, (half, half), 0)
    column = lax.broadcasted_iota(jnp.int32, (half, half), 1)
    lower, upper = row >= column, row <= column

    def tri(x, keep):
        return jnp.where(keep, x, 0.0).astype(BF16)

    q, k, v, g = (all_ref[j, :, at] for j in range(4))
    probe = mm(g, v[up], NT)
    probe = jnp.concatenate([tri(probe[up], lower), probe[down].astype(BF16)], 0)
    first = mm(probe, k[up], NN)
    second = mm(tri(mm(g[down], v[down], NT), lower), k[down], NN)
    yield 0, up, first[up]
    yield 0, down, first[down] + second
    for grad, left, right in ((1, v, g), (2, k, q)):
        other = q if grad == 1 else g
        late = mm(left, right[down], NT)
        late = jnp.concatenate([late[up].astype(BF16), tri(late[down], upper)], 0)
        second = mm(late, other[down], NN)
        first = mm(tri(mm(left[up], right[up], NT), upper), other[up], NN)
        yield grad, up, first + second[up]
        yield grad, down, second[down]


def prefix_suffix(core_ref, mine_ref, other_ref, theirs_ref, j):
    first, mine = core_ref[0] == 0, mine_ref[j]
    other = (other_ref[j].astype(F32) + theirs_ref[j]).astype(BF16)
    return jnp.where(first, mine, other), jnp.where(first, other, mine)


def whole_kernel(peers, aliased, scale, col_ref, core_ref, *refs):
    src, refs = refs[: peers + 1], refs[peers + 1 :]
    owns, got, sums = refs[:4], refs[4 : 4 + peers], refs[4 + peers : 7 + peers]
    outs, all_ref = refs[7 + peers + 3 * aliased : -1], refs[-1]
    gather_rows(src, owns, got, range(4), all_ref)
    for j in range(PAIR // DK):
        at = slice(j * DK, (j + 1) * DK)
        prefix, suffix = prefix_suffix(core_ref, *sums, j)
        for grad, rows, value in within(all_ref, at):
            which, state, dims = ((3, prefix, NT), (2, suffix, NT), (1, suffix, NN))[grad]
            value = value + mm(all_ref[which, rows, at], state, dims)
            outs[grad][rows, at] = (scale * value).astype(BF16)


def within_kernel(peers, aliased, scale, col_ref, core_ref, *refs):
    src, refs = refs[: peers + 1], refs[peers + 1 :]
    owns, got = refs[:4], refs[4 : 4 + peers]
    outs, rows_ref, all_ref = refs[4 + peers + 4 * aliased : -2], refs[-2], refs[-1]
    gather_rows(src, owns, got, range(4), all_ref)
    rows_ref[...] = all_ref[1:]
    for j in range(PAIR // DK):
        at = slice(j * DK, (j + 1) * DK)
        for grad, rows, value in within(all_ref, at):
            outs[grad][rows, at] = value.astype(BF16)


def across_kernel(aliased, scale, core_ref, rows_ref, *refs):
    sums, parts, outs = refs[:3], refs[3:6], refs[6 + 3 * aliased :]
    for j in range(PAIR // DK):
        at = slice(j * DK, (j + 1) * DK)
        prefix, suffix = prefix_suffix(core_ref, *sums, j)
        for grad, (which, state, dims) in enumerate(((2, prefix, NT), (1, suffix, NT), (0, suffix, NN))):
            value = parts[grad][:, at].astype(F32) + mm(rows_ref[which, :, at], state, dims)
            outs[grad][:, at] = (scale * value).astype(BF16)


ANY = pl.BlockSpec(memory_space=pl.ANY)


def outputs(kernel, cols, core, src, arrays, got, sums, first, pairs, base, room, scale, into):
    rows = arrays[0].shape[0]
    total = rows * (1 + len(got))
    whole = kernel is whole_kernel
    own = pl.BlockSpec((rows, PAIR), lambda i, c, *s: (0, c[0] + first + i))
    there = pl.BlockSpec((4, rows, PAIR), lambda i, c, *s: (0, 0, i))
    operands, specs = [*arrays, *got], [own] * 4 + [there] * len(got)
    here = pl.BlockSpec((total, PAIR), lambda i, c, *s: (0, base + i))
    outs, shapes = [here] * 3, [jax.ShapeDtypeStruct((total, room * PAIR), BF16)] * 3
    if whole:
        sums, offset = sums
        operands += sums
        specs += [pl.BlockSpec((PAIR // DK, DK, DK), lambda i, c, *s: (offset + i, 0, 0))] * 3
    else:
        outs.append(pl.BlockSpec((3, total, PAIR), lambda i, c, *s: (0, 0, base + i)))
        shapes.append(jax.ShapeDtypeStruct((3, total, room * PAIR), BF16))
    start = 2 + len(src) + len(operands)
    shared = [] if into is None else list(into)
    return pl.pallas_call(
        functools.partial(kernel, len(got), int(into is not None), scale),
        grid_spec=pltpu.PrefetchScalarGridSpec(
            num_scalar_prefetch=2 + len(src),
            grid=(pairs,),
            in_specs=specs + [ANY] * len(shared),
            out_specs=outs,
            scratch_shapes=[pltpu.VMEM((4, total, PAIR), BF16)],
        ),
        out_shape=shapes,
        input_output_aliases={start + j: j for j in range(len(shared))},
        cost_estimate=cost(14 * total * total * PAIR * pairs, 14 * total * PAIR * pairs),
        compiler_params=pltpu.CompilerParams(vmem_limit_bytes=VMEM_LIMIT),
    )(cols[0], core, *src, *operands, *shared)


def finish(parts, core, sums, pairs, room, scale, into):
    total = parts[0].shape[0]
    here = pl.BlockSpec((total, PAIR), lambda i, d: (0, i))
    shared = [] if into is None else list(into)
    return pl.pallas_call(
        functools.partial(across_kernel, int(into is not None), scale),
        grid_spec=pltpu.PrefetchScalarGridSpec(
            num_scalar_prefetch=1,
            grid=(pairs,),
            in_specs=[
                pl.BlockSpec((3, total, PAIR), lambda i, d: (0, 0, i)),
                *[pl.BlockSpec((PAIR // DK, DK, DK), lambda i, d: (i, 0, 0))] * 3,
                *[here] * 3,
                *[ANY] * len(shared),
            ],
            out_specs=[here] * 3,
        ),
        out_shape=[jax.ShapeDtypeStruct((total, room * PAIR), BF16)] * 3,
        input_output_aliases={8 + j: j for j in range(len(shared))},
        cost_estimate=cost(6 * total * DK * PAIR * pairs, 24 * total * PAIR * pairs),
        compiler_params=pltpu.CompilerParams(vmem_limit_bytes=VMEM_LIMIT),
        name="across",
    )(core, parts[3], *sums, *parts[:3], *shared)


def running_kernel(up_ref, part_ref, out_ref):
    count = part_ref.shape[0]

    def run(order):
        total = jnp.zeros(part_ref.shape[1:], F32)
        for i in order:
            out_ref[i] = total.astype(BF16)
            total = total + part_ref[i].astype(F32)

    @pl.when(up_ref[0] == 1)
    def _():
        run(range(count))

    @pl.when(up_ref[0] == 0)
    def _():
        run(reversed(range(count)))


def deal_and_sum(own, up, groups):
    count = len(groups[0])
    parts = lax.all_to_all(own.reshape(count, -1, DK), "seq", 0, 0, tiled=True, axis_index_groups=groups)
    mine = pl.pallas_call(
        running_kernel,
        in_specs=[pl.BlockSpec(memory_space=pltpu.SMEM), pl.BlockSpec(memory_space=pltpu.VMEM)],
        out_specs=pl.BlockSpec(memory_space=pltpu.VMEM),
        out_shape=jax.ShapeDtypeStruct(parts.shape, BF16),
        cost_estimate=cost(parts.size, 4 * parts.size),
        name="running",
    )(up.astype(jnp.int32).reshape(1), parts)
    mine = lax.all_to_all(mine, "seq", 0, 0, tiled=True, axis_index_groups=groups)
    return mine.reshape(own.shape)


def scan_chips(keep, give):
    count = lax.axis_size("seq")
    swap = [(i, i ^ 1) for i in range(count)]
    chip = keep + lax.ppermute(give, "seq", swap)
    theirs = lax.ppermute(keep, "seq", swap)
    groups = [list(range(core, count, 2)) for core in (0, 1)]
    mine = deal_and_sum(chip.astype(BF16), lax.axis_index("seq") % 2 == 0, groups)
    return mine, lax.ppermute(mine, "seq", swap), theirs


def local(queries, key_vectors, value_vectors, out_grads):
    return grads((queries, key_vectors, value_vectors, out_grads))


def grads(arrays):
    peers = lax.axis_size("head")
    place = lax.axis_index("head")
    rows = arrays[0].shape[0]
    pairs_here = arrays[0].shape[1] // PAIR // peers
    total_tokens = rows * peers * lax.axis_size("seq")
    scale = 1.0 / math.sqrt(DK * total_tokens)
    late = pairs_here // 2
    early = pairs_here - late
    sizes = [1] * early
    split = len(sizes)
    sizes += [n for n in (late - 3 * (late // 4), late // 4, late // 4, late // 4) if n]
    firsts = [sum(sizes[:i]) for i in range(len(sizes))]
    shifts = range(1, peers)
    cols = [jnp.reshape((place + s) % peers * pairs_here, (1,)).astype(jnp.int32) for s in range(peers)]
    src = [jnp.reshape((place - s) % peers, (1,)).astype(jnp.int32) for s in range(peers)]

    def move(values):
        return [
            lax.ppermute(value, "head", [(i, (i + s) % peers) for i in range(peers)])
            for s, value in zip(shifts, values)
        ]

    got = [move(pack(cols, peers, arrays, 0, sizes[:1])[0])]
    late_sent = [states(cols, arrays, [], early, late, BF16, s) for s in shifts]
    late_got = move(late_sent)
    for c, packed in enumerate(pack(cols, peers, arrays, sizes[0], sizes[1:]), 1):
        got.append(move(packed))
    core = (lax.axis_index("seq") % 2).astype(jnp.int32).reshape(1)
    keep, give = split_states(cols, core, arrays, [], early, late, 0, late, None)
    for piece in late_got:
        first, second = jnp.where(core[0] == 0, piece[0], piece[1]), jnp.where(core[0] == 0, piece[1], piece[0])
        keep, give = keep + first.astype(F32), give + second.astype(F32)
    late_sums = scan_chips(keep, give)
    own = parts = None
    for c in range(split):
        own = split_states(cols, core, arrays, got[c], firsts[c], sizes[c], firsts[c], early, own)
    for c in range(split):
        parts = outputs(
            within_kernel, cols, core, src, arrays, got[c], None, firsts[c], sizes[c], firsts[c], early, scale, parts
        )
    early_sums = scan_chips(*own)

    outs = None
    for c in range(split, len(sizes)):
        if c == len(sizes) - 1:
            outs = finish(parts, core, early_sums, early, pairs_here, scale, outs)
        sums = (late_sums, firsts[c] - early)
        outs = outputs(
            whole_kernel, cols, core, src, arrays, got[c], sums, firsts[c], sizes[c], firsts[c], pairs_here, scale, outs
        )
    return tuple(outs)


def solution(mesh):
    tokens = P(("seq", "head"), None)
    return jax.shard_map(
        local,
        mesh=mesh,
        in_specs=(tokens,) * 4,
        out_specs=(P("seq", "head"),) * 3,
        check_vma=False,
    )
```

```python
import functools
import math

import jax
import jax.numpy as jnp
from jax import lax
from jax.experimental import pallas as pl
from jax.experimental.pallas import tpu as pltpu
from jax.sharding import PartitionSpec as P


DK = 128
F32 = jnp.float32
BF16 = jnp.bfloat16
PAIR = 2 * DK
VMEM_LIMIT = 67_000_000


NT = (((1,), (1,)), ((), ()))
TN = (((0,), (0,)), ((), ()))
NN = (((1,), (0,)), ((), ()))


def mm(a, b, dims):
    return lax.dot_general(a, b, dims, preferred_element_type=F32)


def cost(flops, size):
    return pl.CostEstimate(flops=flops, bytes_accessed=size, transcendentals=0)


def pack_kernel(sizes, first, peers, *refs):
    cols, refs = refs[: peers - 1], refs[peers - 1 :]
    count = len(sizes) * (peers - 1)
    ins, outs, bufs = refs[:4], refs[4 : 4 + count], refs[4 + count : 4 + 2 * count]
    in_sem, out_sem = refs[4 + 2 * count :]
    reads, writes = [], []
    for c, n in enumerate(sizes):
        for s in range(peers - 1):
            i = c * (peers - 1) + s
            at = pl.multiple_of((cols[s][0] + (first + sum(sizes[:c]))) * PAIR, PAIR)
            for j in range(4):
                k = 4 * i + j
                reads.append(
                    pltpu.make_async_copy(ins[j].at[:, pl.ds(at, n * PAIR)], bufs[i].at[j], in_sem.at[k])
                )
                writes.append(pltpu.make_async_copy(bufs[i].at[j], outs[i].at[j], out_sem.at[k]))
    for read in reads:
        read.start()
    for read, write in zip(reads, writes):
        read.wait()
        write.start()
    for write in writes:
        write.wait()


def pack(cols, peers, arrays, first, sizes):
    rows = arrays[0].shape[0]
    shapes = [(4, rows, n * PAIR) for n in sizes for _ in range(1, peers)]
    flat = pl.pallas_call(
        functools.partial(pack_kernel, sizes, first, peers),
        in_specs=[pl.BlockSpec(memory_space=pltpu.SMEM)] * (peers - 1) + [pl.BlockSpec(memory_space=pl.ANY)] * 4,
        out_specs=[pl.BlockSpec(memory_space=pl.ANY)] * len(shapes),
        out_shape=[jax.ShapeDtypeStruct(shape, BF16) for shape in shapes],
        scratch_shapes=[pltpu.VMEM(shape, BF16) for shape in shapes]
        + [pltpu.SemaphoreType.DMA((4 * len(shapes),))] * 2,
        cost_estimate=cost(0, 16 * rows * sum(sizes) * PAIR * (peers - 1)),
        name="pack",
    )(*cols[1:], *arrays)
    return [flat[i * (peers - 1) : (i + 1) * (peers - 1)] for i in range(len(sizes))]


def state_kernel(peers, col_ref, q_ref, k_ref, v_ref, g_ref, *rest):
    out_ref = rest[-1]
    for j in range(PAIR // DK):
        at = slice(j * DK, (j + 1) * DK)
        kv = mm(k_ref[:, at], v_ref[:, at], TN)
        qg = mm(q_ref[:, at], g_ref[:, at], TN)
        for r in rest[:peers]:
            kv = kv + mm(r[1, :, at], r[2, :, at], TN)
            qg = qg + mm(r[0, :, at], r[3, :, at], TN)
        out_ref[0, j] = kv.astype(out_ref.dtype)
        out_ref[1, j] = qg.astype(out_ref.dtype)


def states(cols, arrays, got, first, pairs, dtype=BF16, at=0, room=None, base=0, into=None):
    rows = arrays[0].shape[0]
    own = pl.BlockSpec((rows, PAIR), lambda i, c: (0, c[0] + first + i))
    there = pl.BlockSpec((4, rows, PAIR), lambda i, c: (0, 0, i))
    tokens = rows * (1 + len(got))
    per = PAIR // DK
    shared = [] if into is None else [into]
    return pl.pallas_call(
        functools.partial(state_kernel, len(got)),
        grid_spec=pltpu.PrefetchScalarGridSpec(
            num_scalar_prefetch=1,
            grid=(pairs,),
            in_specs=[own] * 4 + [there] * len(got) + [pl.BlockSpec(memory_space=pl.ANY)] * len(shared),
            out_specs=pl.BlockSpec((2, per, DK, DK), lambda i, c: (0, base + i, 0, 0)),
        ),
        out_shape=jax.ShapeDtypeStruct((2, per * (room or pairs), DK, DK), dtype),
        input_output_aliases={5 + len(got): 0} if shared else {},
        cost_estimate=cost(4 * tokens * DK * PAIR * pairs, 8 * tokens * pairs * PAIR),
        compiler_params=pltpu.CompilerParams(vmem_limit_bytes=VMEM_LIMIT),
        name="states",
    )(cols[at], *arrays, *got, *shared)


def split_kernel(peers, col_ref, core_ref, q_ref, k_ref, v_ref, g_ref, *rest):
    keep_ref, give_ref = rest[-2:]
    first = core_ref[0] == 0
    for j in range(PAIR // DK):
        at = slice(j * DK, (j + 1) * DK)
        kv = mm(k_ref[:, at], v_ref[:, at], TN)
        qg = mm(q_ref[:, at], g_ref[:, at], TN)
        for r in rest[:peers]:
            kv = kv + mm(r[1, :, at], r[2, :, at], TN)
            qg = qg + mm(r[0, :, at], r[3, :, at], TN)
        keep_ref[j] = jnp.where(first, kv, qg).astype(keep_ref.dtype)
        give_ref[j] = jnp.where(first, qg, kv).astype(give_ref.dtype)


def split_states(cols, core, arrays, got, first, pairs, base, room, into, dtype):
    rows = arrays[0].shape[0]
    own = pl.BlockSpec((rows, PAIR), lambda i, c, d: (0, c[0] + first + i))
    there = pl.BlockSpec((4, rows, PAIR), lambda i, c, d: (0, 0, i))
    tokens = rows * (1 + len(got))
    per = PAIR // DK
    shared = [] if into is None else list(into)
    return pl.pallas_call(
        functools.partial(split_kernel, len(got)),
        grid_spec=pltpu.PrefetchScalarGridSpec(
            num_scalar_prefetch=2,
            grid=(pairs,),
            in_specs=[own] * 4 + [there] * len(got) + [pl.BlockSpec(memory_space=pl.ANY)] * len(shared),
            out_specs=[pl.BlockSpec((per, DK, DK), lambda i, c, d: (base + i, 0, 0))] * 2,
        ),
        out_shape=[jax.ShapeDtypeStruct((per * room, DK, DK), dtype)] * 2,
        input_output_aliases={6 + len(got) + j: j for j in range(len(shared))},
        cost_estimate=cost(4 * tokens * DK * PAIR * pairs, 8 * tokens * pairs * PAIR),
        compiler_params=pltpu.CompilerParams(vmem_limit_bytes=VMEM_LIMIT),
        name="split_states",
    )(cols[0], core, *arrays, *got, *shared)


def gather_rows(src, owns, got, which, all_ref):
    rows = owns[0].shape[0]
    mine = pl.multiple_of(src[0][0] * rows, rows)
    for j in which:
        all_ref[j, pl.ds(mine, rows), :] = owns[j][...]
    for p, r in enumerate(got):
        at = pl.multiple_of(src[p + 1][0] * rows, rows)
        for j in which:
            all_ref[j, pl.ds(at, rows), :] = r[j]


def within(all_ref, at):
    total = all_ref.shape[1]
    half = total // 2
    up, down = slice(0, half), slice(half, total)
    row = lax.broadcasted_iota(jnp.int32, (half, half), 0)
    column = lax.broadcasted_iota(jnp.int32, (half, half), 1)
    lower, upper = row >= column, row <= column

    def tri(x, keep):
        return jnp.where(keep, x, 0.0).astype(BF16)

    q, k, v, g = (all_ref[j, :, at] for j in range(4))
    probe = mm(g, v[up], NT)
    probe = jnp.concatenate([tri(probe[up], lower), probe[down].astype(BF16)], 0)
    first = mm(probe, k[up], NN)
    second = mm(tri(mm(g[down], v[down], NT), lower), k[down], NN)
    yield 0, up, first[up]
    yield 0, down, first[down] + second
    for grad, left, right in ((1, v, g), (2, k, q)):
        other = q if grad == 1 else g
        late = mm(left, right[down], NT)
        late = jnp.concatenate([late[up].astype(BF16), tri(late[down], upper)], 0)
        second = mm(late, other[down], NN)
        first = mm(tri(mm(left[up], right[up], NT), upper), other[up], NN)
        yield grad, up, first + second[up]
        yield grad, down, second[down]


def prefix_suffix(core_ref, mine_ref, other_ref, theirs_ref, j):
    first, mine = core_ref[0] == 0, mine_ref[j]
    other = (other_ref[j].astype(F32) + theirs_ref[j].astype(F32)).astype(BF16)
    return jnp.where(first, mine, other), jnp.where(first, other, mine)


def whole_kernel(peers, aliased, scale, col_ref, core_ref, *refs):
    src, refs = refs[: peers + 1], refs[peers + 1 :]
    owns, got, sums = refs[:4], refs[4 : 4 + peers], refs[4 + peers : 7 + peers]
    outs, all_ref = refs[7 + peers + 3 * aliased : -1], refs[-1]
    gather_rows(src, owns, got, range(4), all_ref)
    for j in range(PAIR // DK):
        at = slice(j * DK, (j + 1) * DK)
        prefix, suffix = prefix_suffix(core_ref, *sums, j)
        for grad, rows, value in within(all_ref, at):
            which, state, dims = ((3, prefix, NT), (2, suffix, NT), (1, suffix, NN))[grad]
            value = value + mm(all_ref[which, rows, at], state, dims)
            outs[grad][rows, at] = (scale * value).astype(BF16)


def within_kernel(peers, aliased, scale, col_ref, core_ref, *refs):
    src, refs = refs[: peers + 1], refs[peers + 1 :]
    owns, got = refs[:4], refs[4 : 4 + peers]
    outs, rows_ref, all_ref = refs[4 + peers + 4 * aliased : -2], refs[-2], refs[-1]
    gather_rows(src, owns, got, range(4), all_ref)
    rows_ref[...] = all_ref[1:]
    for j in range(PAIR // DK):
        at = slice(j * DK, (j + 1) * DK)
        for grad, rows, value in within(all_ref, at):
            outs[grad][rows, at] = value.astype(BF16)


def across_kernel(aliased, scale, core_ref, rows_ref, *refs):
    sums, parts, outs = refs[:3], refs[3:6], refs[6 + 3 * aliased :]
    for j in range(PAIR // DK):
        at = slice(j * DK, (j + 1) * DK)
        prefix, suffix = prefix_suffix(core_ref, *sums, j)
        for grad, (which, state, dims) in enumerate(((2, prefix, NT), (1, suffix, NT), (0, suffix, NN))):
            value = parts[grad][:, at].astype(F32) + mm(rows_ref[which, :, at], state, dims)
            outs[grad][:, at] = (scale * value).astype(BF16)


ANY = pl.BlockSpec(memory_space=pl.ANY)


def outputs(kernel, cols, core, src, arrays, got, sums, first, pairs, base, room, scale, into):
    rows = arrays[0].shape[0]
    total = rows * (1 + len(got))
    whole = kernel is whole_kernel
    own = pl.BlockSpec((rows, PAIR), lambda i, c, *s: (0, c[0] + first + i))
    there = pl.BlockSpec((4, rows, PAIR), lambda i, c, *s: (0, 0, i))
    operands, specs = [*arrays, *got], [own] * 4 + [there] * len(got)
    here = pl.BlockSpec((total, PAIR), lambda i, c, *s: (0, base + i))
    outs, shapes = [here] * 3, [jax.ShapeDtypeStruct((total, room * PAIR), BF16)] * 3
    if whole:
        sums, offset = sums
        operands += sums
        specs += [pl.BlockSpec((PAIR // DK, DK, DK), lambda i, c, *s: (offset + i, 0, 0))] * 3
    else:
        outs.append(pl.BlockSpec((3, total, PAIR), lambda i, c, *s: (0, 0, base + i)))
        shapes.append(jax.ShapeDtypeStruct((3, total, room * PAIR), BF16))
    start = 2 + len(src) + len(operands)
    shared = [] if into is None else list(into)
    return pl.pallas_call(
        functools.partial(kernel, len(got), int(into is not None), scale),
        grid_spec=pltpu.PrefetchScalarGridSpec(
            num_scalar_prefetch=2 + len(src),
            grid=(pairs,),
            in_specs=specs + [ANY] * len(shared),
            out_specs=outs,
            scratch_shapes=[pltpu.VMEM((4, total, PAIR), BF16)],
        ),
        out_shape=shapes,
        input_output_aliases={start + j: j for j in range(len(shared))},
        cost_estimate=cost(14 * total * total * PAIR * pairs, 14 * total * PAIR * pairs),
        compiler_params=pltpu.CompilerParams(vmem_limit_bytes=VMEM_LIMIT),
    )(cols[0], core, *src, *operands, *shared)


def finish(parts, core, sums, pairs, room, scale, into):
    total = parts[0].shape[0]
    here = pl.BlockSpec((total, PAIR), lambda i, d: (0, i))
    shared = [] if into is None else list(into)
    return pl.pallas_call(
        functools.partial(across_kernel, int(into is not None), scale),
        grid_spec=pltpu.PrefetchScalarGridSpec(
            num_scalar_prefetch=1,
            grid=(pairs,),
            in_specs=[
                pl.BlockSpec((3, total, PAIR), lambda i, d: (0, 0, i)),
                *[pl.BlockSpec((PAIR // DK, DK, DK), lambda i, d: (i, 0, 0))] * 3,
                *[here] * 3,
                *[ANY] * len(shared),
            ],
            out_specs=[here] * 3,
        ),
        out_shape=[jax.ShapeDtypeStruct((total, room * PAIR), BF16)] * 3,
        input_output_aliases={8 + j: j for j in range(len(shared))},
        cost_estimate=cost(6 * total * DK * PAIR * pairs, 24 * total * PAIR * pairs),
        compiler_params=pltpu.CompilerParams(vmem_limit_bytes=VMEM_LIMIT),
        name="across",
    )(core, parts[3], *sums, *parts[:3], *shared)


def running_kernel(up_ref, part_ref, out_ref):
    count = part_ref.shape[0]

    def run(order):
        total = jnp.zeros(part_ref.shape[1:], F32)
        for i in order:
            out_ref[i] = total.astype(BF16)
            total = total + part_ref[i].astype(F32)

    @pl.when(up_ref[0] == 1)
    def _():
        run(range(count))

    @pl.when(up_ref[0] == 0)
    def _():
        run(reversed(range(count)))


def deal_and_sum(own, up, groups):
    count = len(groups[0])
    parts = lax.all_to_all(own.reshape(count, -1, DK), "seq", 0, 0, tiled=True, axis_index_groups=groups)
    mine = pl.pallas_call(
        running_kernel,
        in_specs=[pl.BlockSpec(memory_space=pltpu.SMEM), pl.BlockSpec(memory_space=pltpu.VMEM)],
        out_specs=pl.BlockSpec(memory_space=pltpu.VMEM),
        out_shape=jax.ShapeDtypeStruct(parts.shape, BF16),
        cost_estimate=cost(parts.size, 4 * parts.size),
        name="running",
    )(up.astype(jnp.int32).reshape(1), parts)
    mine = lax.all_to_all(mine, "seq", 0, 0, tiled=True, axis_index_groups=groups)
    return mine.reshape(own.shape)


def scan_chips(keep, give):
    count = lax.axis_size("seq")
    swap = [(i, i ^ 1) for i in range(count)]
    chip = keep.astype(F32) + lax.ppermute(give, "seq", swap).astype(F32)
    theirs = lax.ppermute(keep, "seq", swap)
    groups = [list(range(core, count, 2)) for core in (0, 1)]
    mine = deal_and_sum(chip.astype(BF16), lax.axis_index("seq") % 2 == 0, groups)
    return mine, lax.ppermute(mine, "seq", swap), theirs


def local(queries, key_vectors, value_vectors, out_grads):
    return grads((queries, key_vectors, value_vectors, out_grads))


def grads(arrays):
    peers = lax.axis_size("head")
    place = lax.axis_index("head")
    rows = arrays[0].shape[0]
    pairs_here = arrays[0].shape[1] // PAIR // peers
    total_tokens = rows * peers * lax.axis_size("seq")
    scale = 1.0 / math.sqrt(DK * total_tokens)
    late = pairs_here // 2
    early = pairs_here - late
    sizes = [1] * early
    split = len(sizes)
    sizes += [n for n in (late - 2 * (late // 4), late // 4, late // 4) if n]
    firsts = [sum(sizes[:i]) for i in range(len(sizes))]
    shifts = range(1, peers)
    cols = [jnp.reshape((place + s) % peers * pairs_here, (1,)).astype(jnp.int32) for s in range(peers)]
    src = [jnp.reshape((place - s) % peers, (1,)).astype(jnp.int32) for s in range(peers)]

    def move(values):
        return [
            lax.ppermute(value, "head", [(i, (i + s) % peers) for i in range(peers)])
            for s, value in zip(shifts, values)
        ]

    got = [move(pack(cols, peers, arrays, 0, sizes[:1])[0])]
    late_sent = [states(cols, arrays, [], early, late, BF16, s) for s in shifts]
    late_got = move(late_sent)
    for c, packed in enumerate(pack(cols, peers, arrays, sizes[0], sizes[1:]), 1):
        got.append(move(packed))
    core = (lax.axis_index("seq") % 2).astype(jnp.int32).reshape(1)
    keep, give = split_states(cols, core, arrays, [], early, late, 0, late, None, F32)
    for piece in late_got:
        first, second = jnp.where(core[0] == 0, piece[0], piece[1]), jnp.where(core[0] == 0, piece[1], piece[0])
        keep, give = keep + first.astype(F32), give + second.astype(F32)
    late_sums = scan_chips(keep, give)
    own = parts = None
    for c in range(split):
        own = split_states(cols, core, arrays, got[c], firsts[c], sizes[c], firsts[c], early, own, BF16)
    for c in range(split):
        parts = outputs(
            within_kernel, cols, core, src, arrays, got[c], None, firsts[c], sizes[c], firsts[c], early, scale, parts
        )
    early_sums = scan_chips(*own)

    outs = None
    for c in range(split, len(sizes)):
        if c == len(sizes) - 1:
            outs = finish(parts, core, early_sums, early, pairs_here, scale, outs)
        sums = (late_sums, firsts[c] - early)
        outs = outputs(
            whole_kernel, cols, core, src, arrays, got[c], sums, firsts[c], sizes[c], firsts[c], pairs_here, scale, outs
        )
    return tuple(outs)


def solution(mesh):
    tokens = P(("seq", "head"), None)
    return jax.shard_map(
        local,
        mesh=mesh,
        in_specs=(tokens,) * 4,
        out_specs=(P("seq", "head"),) * 3,
        check_vma=False,
    )
```
